32 devices in a mesh: groups: 2 (over x), seq: 16 (over z, y, core).
Axes of the slice: x: 2, y: 2, z: 4, core: 2. Of those that a mesh axis runs over, the one named last changes fastest.
Arguments:
- query_rows: bfloat16 [16384, 1024], P(('groups', 'seq')), parts along dimension 0, may hold values from -6 to 6
- key_rows: bfloat16 [16384, 1024], P(('groups', 'seq')), parts along dimension 0, may hold values from -6 to 6
- value_rows: bfloat16 [16384, 1024], P(('groups', 'seq')), parts along dimension 0, may hold values from -6 to 6
- log_decay: float32 [8, 16384], P(None, ('groups', 'seq')), parts along dimension 1
- run_start: int32 [16384], P(('groups', 'seq')), parts along dimension 0, may hold values 0 or 1
- out_grad: bfloat16 [16384, 1024], P(('groups', 'seq')), parts along dimension 0, may hold values from -6 to 6
Outputs:
- attended: bfloat16 [16384, 1024], P(('groups', 'seq')), parts along dimension 0
- query_grad: bfloat16 [16384, 1024], P(('groups', 'seq')), parts along dimension 0
- key_grad: bfloat16 [16384, 1024], P(('groups', 'seq')), parts along dimension 0
- value_grad: bfloat16 [16384, 1024], P(('groups', 'seq')), parts along dimension 0
The draws below stay inside these ranges and needn't reach their ends.
There are 2 independent parts, one for each index of `groups`. The reference program is written for one: setup_inputs(seed, part) draws one part's arguments, and reference() takes and returns one part's arrays. A program takes and returns all parts, laid end to end along the dimension named above; each array names one. Nothing has to cross between parts.
Inputs may be any that keep to these rules, and one draw needn't show every extreme that they name: `run_start`: 1 marks a position at which a new run begins and the state starts afresh.
All inputs are finite; a program needn't handle non-finite values. No bound on the sum of `run_start` on one device may be relied on, other than what follows from the above.
Results may differ from the reference program's by a relative error of at most 0.0086.
Values sent between devices are 32-bit elements; how exact they have to be, the bound alone decides.
No kernel may reach another device: no remote copies, remote signals or barrier semaphores. Data moves between devices by JAX's collectives and lax.ppermute only.
A program may use at most 128 MiB of HBM per device.

```python
import math
import jax
import jax.numpy as jnp
from jax import lax

HEADS_PER_SHARD = 8
DH = 128
BLOCK = 256
TOKENS_PER_SHARD = 512
SEQUENCE_TOKENS = 8192
WIDTH = 1024


def draw_log_decay(key, part):
    key_rows_divided = jax.random.split(key, 9)
    device_number = SEQUENCE_TOKENS // TOKENS_PER_SHARD
    ranking = jax.random.permutation(key_rows_divided[0], HEADS_PER_SHARD)
    slow_count = max(HEADS_PER_SHARD // 2, 1)
    slow_heads = ranking < slow_count
    token_locations = jnp.arange(SEQUENCE_TOKENS)
    owning_device = token_locations // TOKENS_PER_SHARD
    slower_decay_base = jax.random.uniform(key_rows_divided[1], (HEADS_PER_SHARD,), jnp.float32, 0.02, 0.08) * (math.log(10.0) / SEQUENCE_TOKENS)
    run_device_index = jax.random.randint(key_rows_divided[6], (HEADS_PER_SHARD,), 0, device_number)
    run_token_total = jax.random.uniform(key_rows_divided[7], (HEADS_PER_SHARD,), jnp.float32, 0.3, 0.7)
    within_run = (owning_device[None, :] == run_device_index[:, None]).astype(jnp.float32)
    slower_decay_rate = slower_decay_base[:, None] + within_run * (run_token_total[:, None] / TOKENS_PER_SHARD)
    fast_base = math.log(10.0) / jax.random.uniform(key_rows_divided[2], (HEADS_PER_SHARD,), jnp.float32, 30.0, 50.0)
    level_pick = jax.random.randint(key_rows_divided[8], (HEADS_PER_SHARD, device_number), 0, 2)
    device_level = jnp.where(level_pick == 1, 1.0, 0.002).astype(jnp.float32)
    level_at = jnp.take(device_level, owning_device, axis=1)
    fast_rate = fast_base[:, None] * level_at
    default_decay_rate = jnp.where(slow_heads[:, None], slower_decay_rate, fast_rate)
    decay_multiplier = jnp.exp(jax.random.uniform(key_rows_divided[3], (HEADS_PER_SHARD, SEQUENCE_TOKENS), jnp.float32, -math.log(2.0), math.log(2.0)))
    reset_positions = jax.random.randint(key_rows_divided[4], (HEADS_PER_SHARD, 2), 0, SEQUENCE_TOKENS)
    loss_values = jnp.log(jax.random.uniform(key_rows_divided[5], (HEADS_PER_SHARD, 2), jnp.float32, 0.6, 0.8))
    reset_events = jnp.sum(jnp.where(token_locations[None, None, :] == reset_positions[:, :, None], loss_values[:, :, None], 0.0), axis=1)
    return -default_decay_rate * decay_multiplier + reset_events


def touch_ends(values, rng, smallest, top_value):
    longest = values.shape.index(max(values.shape))
    spots = []
    for shift in (0, 1):
        where = [jax.random.randint(jax.random.fold_in(rng, axis), (), 0, length) for axis, length in enumerate(values.shape)]
        where[longest] = (where[longest] + shift) % values.shape[longest]
        spots.append(tuple(where))
    return values.at[spots[0]].set(smallest).at[spots[1]].set(top_value)


def levels(rng, dims, cuts, low, high):
    loudness = 1.0
    for axis_at, shards_of in cuts:
        heights = jax.random.uniform(jax.random.fold_in(jax.random.fold_in(rng, 6), axis_at), (shards_of,), jnp.float32, low / len(cuts), high / len(cuts))
        loudness = loudness * jnp.repeat(jnp.exp(heights), dims[axis_at] // shards_of).reshape((-1,) + (1,) * (len(dims) - 1 - axis_at))
    return loudness


def normal_values(own_key, dims, scale, limit, shards=(), kind=jnp.bfloat16):
    values = scale * jax.random.normal(own_key, dims, jnp.float32)
    if shards:
        values = values * levels(own_key, dims, shards, -0.22, 0.18)
    return jnp.clip(values, -limit, limit).astype(kind)


def setup_inputs(seed: int = 0, part: int = 0) -> dict:
    key_list = jax.random.split(jax.random.key(seed), 7)
    part_splits = jax.random.split(jax.random.fold_in(key_list[6], part), 7)
    return {
        "query_rows": normal_values(part_splits[0], (SEQUENCE_TOKENS, WIDTH), 1.0, 6.0, ((0, 16),)),
        "key_rows": normal_values(part_splits[1], (SEQUENCE_TOKENS, WIDTH), 1.0, 6.0, ((0, 16),)),
        "value_rows": normal_values(part_splits[2], (SEQUENCE_TOKENS, WIDTH), 1.0, 6.0, ((0, 16),)),
        "log_decay": draw_log_decay(jax.random.fold_in(jax.random.fold_in(key_list[6], part), 71), part),
        "run_start": touch_ends((jax.random.randint(part_splits[4], (SEQUENCE_TOKENS,), 0, 16 * TOKENS_PER_SHARD) < 1).astype(jnp.int32), jax.random.fold_in(part_splits[4], 1), 0, 1),
        "out_grad": normal_values(part_splits[5], (SEQUENCE_TOKENS, WIDTH), 1.0, 6.0, ((0, 16),)),
    }


norm_eps = 1e-05

def rounded(values_in):
    return lax.optimization_barrier(values_in.astype(jnp.bfloat16)).astype(jnp.float32)

def block_terms(decays, starts):
    cumulative = jnp.cumsum(decays, axis=-1)
    run_counts = jnp.cumsum(starts, axis=-1, dtype=jnp.int32)
    untouched = (run_counts == 0).astype(jnp.float32)
    entering = jnp.exp(cumulative) * untouched[..., None, :]
    closing = cumulative[..., -1:]
    same_tail = (run_counts == run_counts[..., -1:]).astype(jnp.float32)
    leaving = jnp.exp(closing - cumulative) * same_tail[..., None, :]
    carry_keep = jnp.exp(closing[..., 0]) * untouched[..., -1:]
    differences = cumulative[..., :, None] - cumulative[..., None, :]
    token_locations = jnp.arange(starts.shape[-1])
    permitted = (token_locations[:, None] >= token_locations[None, :]) & (run_counts[..., :, None] == run_counts[..., None, :])
    decay_grid = jnp.where(permitted[..., None, :, :], jnp.exp(jnp.minimum(differences, 0.0)), 0.0)
    return (entering, leaving, carry_keep, decay_grid)

def reference(query_rows, key_rows, value_rows, log_decay, run_start, out_grad):
    blocks = SEQUENCE_TOKENS // BLOCK
    shape_four = (blocks, BLOCK, HEADS_PER_SHARD, DH)
    queries = query_rows.reshape(shape_four)
    keys_all = key_rows.reshape(shape_four)
    values_all = value_rows.reshape(shape_four)
    grads_all = out_grad.reshape(shape_four)
    decays = jnp.swapaxes(log_decay.reshape(HEADS_PER_SHARD, blocks, BLOCK), 0, 1)
    starts = run_start.reshape(blocks, BLOCK)

    def forward_step(state_now, inputs):
        query_block, key_block, value_block, decay_block, start_block, grad_block = inputs
        entering, leaving, carry_keep, decay_grid = block_terms(decay_block, start_block)
        query_wide = query_block.astype(jnp.float32)
        key_wide = key_block.astype(jnp.float32)
        value_wide = value_block.astype(jnp.float32)
        scores = jnp.einsum('thd,shd->hts', query_wide, key_wide)
        weighted = rounded(scores * decay_grid)
        within = jnp.einsum('hts,shd->thd', weighted, value_wide)
        state_low = state_now.astype(jnp.bfloat16)
        state_back = lax.optimization_barrier(state_low).astype(jnp.float32)
        carried = jnp.einsum('thd,hde->the', query_wide, state_back) * entering.T[:, :, None]
        mixture = within + carried
        inverse_rms = lax.rsqrt(lax.optimization_barrier(jnp.mean(mixture * mixture, axis=-1, keepdims=True)) + norm_eps)
        normed = mixture * inverse_rms
        grad_wide = grad_block.astype(jnp.float32)
        mixture_grad = inverse_rms * (grad_wide - normed * lax.optimization_barrier(jnp.mean(grad_wide * normed, axis=-1, keepdims=True)))
        key_scaled = rounded(key_wide * leaving.T[:, :, None])
        state_next = carry_keep[:, None, None] * state_now + jnp.einsum('shd,she->hde', key_scaled, value_wide)
        return (state_next, (normed.astype(jnp.bfloat16), mixture_grad.astype(jnp.bfloat16), state_low))
    start_state = jnp.zeros((HEADS_PER_SHARD, DH, DH), jnp.float32)
    _, (attended, mixture_low, states_low) = lax.scan(forward_step, start_state, (queries, keys_all, values_all, decays, starts, grads_all))

    def backward_step(after_now, inputs):
        query_block, key_block, value_block, decay_block, start_block, grad_low, state_low = inputs
        entering, leaving, carry_keep, decay_grid = block_terms(decay_block, start_block)
        query_wide = query_block.astype(jnp.float32)
        key_wide = key_block.astype(jnp.float32)
        value_wide = value_block.astype(jnp.float32)
        grad_wide = grad_low.astype(jnp.float32)
        state_wide = state_low.astype(jnp.float32)
        enter_rows = entering.T[:, :, None]
        leave_rows = leaving.T[:, :, None]
        scores = jnp.einsum('thd,shd->hts', query_wide, key_wide)
        weighted = rounded(scores * decay_grid)
        prob_grad = jnp.einsum('the,she->hts', grad_wide, value_wide)
        masked_grad = rounded(prob_grad * decay_grid)
        after_wide = rounded(after_now)
        query_part = jnp.einsum('hts,shd->thd', masked_grad, key_wide) + jnp.einsum('the,hde->thd', grad_wide, state_wide) * enter_rows
        key_part = jnp.einsum('hts,thd->shd', masked_grad, query_wide) + jnp.einsum('she,hde->shd', value_wide, after_wide) * leave_rows
        value_part = jnp.einsum('hts,the->she', weighted, grad_wide) + jnp.einsum('shd,hde->she', key_wide, after_wide) * leave_rows
        query_scaled = rounded(query_wide * enter_rows)
        before = carry_keep[:, None, None] * after_now + jnp.einsum('thd,the->hde', query_scaled, grad_wide)
        return (before, (query_part.astype(jnp.bfloat16), key_part.astype(jnp.bfloat16), value_part.astype(jnp.bfloat16)))
    _, (query_grad, key_grad, value_grad) = lax.scan(backward_step, start_state, (queries, keys_all, values_all, decays, starts, mixture_low, states_low), reverse=True)
    flat_shape = (SEQUENCE_TOKENS, HEADS_PER_SHARD * DH)
    return (attended.reshape(flat_shape), query_grad.reshape(flat_shape), key_grad.reshape(flat_shape), value_grad.reshape(flat_shape))
```

```python
import functools

import jax
import jax.numpy as jnp
from jax import lax
from jax.experimental import pallas as pl
from jax.experimental.pallas import tpu as pltpu
from jax.sharding import PartitionSpec as P

BLOCK = 256
DH = 128
EPS = 1e-05
F32 = jnp.float32
BF16 = jnp.bfloat16

NN = (((1,), (0,)), ((), ()))
NT = (((1,), (1,)), ((), ()))
TN = (((0,), (0,)), ((), ()))


def mm(a, b, dims=NN):
    return lax.dot_general(a, b, dims, preferred_element_type=F32)


def whole(shape):
    return pl.BlockSpec(shape, lambda *_: (0,) * len(shape))


def prepare(decay_ref, start_ref, rows_ref, cols_ref):
    tri = (
        lax.broadcasted_iota(jnp.int32, (BLOCK, BLOCK), 0)
        <= lax.broadcasted_iota(jnp.int32, (BLOCK, BLOCK), 1)
    ).astype(F32)
    for b in range(decay_ref.shape[1] // BLOCK):
        at = pl.ds(b * BLOCK, BLOCK)
        starts = jnp.broadcast_to(start_ref[:, at].astype(F32), (8, BLOCK))
        both = jnp.concatenate([decay_ref[:, at], starts], axis=0)
        sums = lax.dot_general(
            both, tri, NN, precision=lax.Precision.HIGHEST, preferred_element_type=F32
        )
        cumul, marks = sums[:8], sums[8:]
        last, last_mark = cumul[:, BLOCK - 1 :], marks[:, BLOCK - 1 :]
        rows_ref[0:8, at] = cumul
        rows_ref[8:16, at] = jnp.where(marks == 0.0, jnp.exp(cumul), 0.0)
        rows_ref[16:24, at] = jnp.where(marks == last_mark, jnp.exp(last - cumul), 0.0)
        rows_ref[24:32, at] = marks
        block = jnp.concatenate([rows_ref[:, at], jnp.zeros((96, BLOCK), F32)], axis=0)
        cols_ref[at, :] = block.T


def put_message(own_ref, send_ref, group, k, j, value, keep):
    body = 2 * k * DH

    @pl.when(group < 2)
    def _():
        at = group * k + j
        own_ref[pl.ds(pl.multiple_of(at * DH, DH), DH), :] = value
        own_ref[pl.ds(body + at, 1), :] = keep

    @pl.when(group >= 2)
    def _():
        at = (group - 2) * k + j
        send_ref[pl.ds(pl.multiple_of(at * DH, DH), DH), :] = value
        send_ref[pl.ds(body + at, 1), :] = keep


def keeps(rows_ref, head):
    enter = rows_ref[pl.ds(8 + head, 1), :]
    k0 = jnp.broadcast_to(enter[:, BLOCK - 1 : BLOCK], (1, DH))
    k1 = jnp.broadcast_to(enter[:, 2 * BLOCK - 1 : 2 * BLOCK], (1, DH))
    return k0, k1


def k1_body(k, info, key_ref, value_ref, decay_ref, start_ref, own_ref, send_ref, loc_ref, rows_ref, cols_ref):
    g = pl.program_id(0)

    @pl.when(g == 0)
    def _():
        prepare(decay_ref, start_ref, rows_ref, cols_ref)
        own_ref[pl.ds(2 * k * DH, 8), :] = jnp.ones((8, DH), F32)
        send_ref[pl.ds(2 * k * DH, 8), :] = jnp.ones((8, DH), F32)

    base = (g ^ info[0]) * k
    for j in range(k):
        head = base + j
        cut = slice(j * DH, (j + 1) * DH)
        leave = rows_ref[pl.ds(16 + head, 1), :]
        terms = []
        for b in range(2):
            rows = slice(b * BLOCK, (b + 1) * BLOCK)
            keys = key_ref[rows, cut].T.astype(F32)
            scaled = (keys * leave[:, rows]).astype(BF16)
            terms.append(mm(scaled, value_ref[rows, cut]))
        k0, k1 = keeps(rows_ref, head)
        loc_ref[j] = terms[0]
        put_message(own_ref, send_ref, g, k, j, k1 * terms[0] + terms[1], k0 * k1)


def k2_body(query_ref, key_ref, value_ref, rows_ref, cols_ref, within_ref, weighted_ref):
    head = pl.program_id(0)
    lane = lax.broadcasted_iota(jnp.int32, (1, DH), 1) == head
    lower = lax.broadcasted_iota(jnp.int32, (BLOCK, BLOCK), 0) >= lax.broadcasted_iota(
        jnp.int32, (BLOCK, BLOCK), 1
    )
    for b in range(2):
        rows = slice(b * BLOCK, (b + 1) * BLOCK)
        grid = grid_of(rows_ref, cols_ref, head, lane, lower, rows)
        scores = mm(query_ref[rows, :], key_ref[rows, :], NT)
        weighted = (scores * grid).astype(BF16)
        weighted_ref[b] = weighted
        within_ref[rows, :] = mm(weighted, value_ref[rows, :])


def column(cols_ref, rows, lane):
    return jnp.sum(jnp.where(lane, cols_ref[rows, :], 0.0), axis=1, keepdims=True)


def grid_of(rows_ref, cols_ref, head, lane, lower, rows):
    cum_row = rows_ref[pl.ds(head, 1), rows]
    mark_row = rows_ref[24:25, rows]
    cum_col = column(cols_ref, rows, lane)
    mark_col = cols_ref[rows, 24:25]
    allowed = lower & (mark_col == mark_row)
    return jnp.where(allowed, jnp.exp(jnp.minimum(cum_col - cum_row, 0.0)), 0.0)


def pick(own_ref, other_ref, g, k, j):
    at = pl.ds(pl.multiple_of(((g & 1) * k + j) * DH, DH), DH)
    return jnp.where(g < 2, own_ref[at, :], other_ref[at, :])


def k3_body(k, info, query_ref, grad_ref, within_ref, loc_ref, rows_ref, cols_ref, mine_ref, other_ref,
            attended_ref, mixgrad_ref, states_ref, own_ref, send_ref, back_ref):
    g = pl.program_id(0)

    @pl.when(g == 0)
    def _():
        own_ref[pl.ds(2 * k * DH, 8), :] = jnp.ones((8, DH), F32)
        send_ref[pl.ds(2 * k * DH, 8), :] = jnp.ones((8, DH), F32)

    base = (g ^ info[0]) * k
    for j in range(k):
        head = base + j
        cut = slice(j * DH, (j + 1) * DH)
        lane = lax.broadcasted_iota(jnp.int32, (1, DH), 1) == 8 + head
        k0, k1 = keeps(rows_ref, head)
        incoming = pick(mine_ref, other_ref, g, k, j)
        states = (incoming, k0 * incoming + loc_ref[j])
        backs = []
        for b in range(2):
            rows = slice(b * BLOCK, (b + 1) * BLOCK)
            low = states[b].astype(BF16)
            states_ref[j, b] = low
            enter = column(cols_ref, rows, lane)
            query = query_ref[rows, cut]
            mixture = within_ref[rows, cut] + mm(query, low) * enter
            inverse = lax.rsqrt(jnp.mean(mixture * mixture, axis=1, keepdims=True) + EPS)
            normed = mixture * inverse
            attended_ref[rows, cut] = normed.astype(BF16)
            wide = grad_ref[rows, cut].astype(F32)
            mixgrad = (inverse * (wide - normed * jnp.mean(wide * normed, axis=1, keepdims=True))).astype(BF16)
            mixgrad_ref[rows, cut] = mixgrad
            scaled = (query.astype(F32) * enter).astype(BF16)
            backs.append(mm(scaled, mixgrad, TN))
        back_ref[j] = backs[1]
        put_message(own_ref, send_ref, g, k, j, k0 * backs[1] + backs[0], k0 * k1)


def k4_body(query_ref, key_ref, value_ref, mixgrad_ref, weighted_ref, states_ref, rows_ref, cols_ref,
            query_grad_ref, key_part_ref, value_part_ref):
    head = pl.program_id(0)
    iota = lax.broadcasted_iota(jnp.int32, (1, DH), 1)
    lower = lax.broadcasted_iota(jnp.int32, (BLOCK, BLOCK), 0) >= lax.broadcasted_iota(
        jnp.int32, (BLOCK, BLOCK), 1
    )
    for b in range(2):
        rows = slice(b * BLOCK, (b + 1) * BLOCK)
        grid = grid_of(rows_ref, cols_ref, head, iota == head, lower, rows)
        mixgrad = mixgrad_ref[rows, :]
        masked = (mm(mixgrad, value_ref[rows, :], NT) * grid).astype(BF16)
        enter = column(cols_ref, rows, iota == 8 + head)
        query_grad_ref[rows, :] = (
            mm(masked, key_ref[rows, :]) + mm(mixgrad, states_ref[0, b], NT) * enter
        ).astype(BF16)
        key_part_ref[rows, :] = mm(masked, query_ref[rows, :], TN)
        value_part_ref[rows, :] = mm(weighted_ref[b], mixgrad, TN)


def k5_body(k, info, key_ref, value_ref, key_part_ref, value_part_ref, back_ref, rows_ref, cols_ref, mine_ref,
            other_ref, key_grad_ref, value_grad_ref):
    g = pl.program_id(0)
    base = (g ^ info[0]) * k
    for j in range(k):
        head = base + j
        cut = slice(j * DH, (j + 1) * DH)
        lane = lax.broadcasted_iota(jnp.int32, (1, DH), 1) == 16 + head
        k0, k1 = keeps(rows_ref, head)
        outgoing = pick(mine_ref, other_ref, g, k, j)
        afters = (k1 * outgoing + back_ref[j], outgoing)
        for b in range(2):
            rows = slice(b * BLOCK, (b + 1) * BLOCK)
            low = afters[b].astype(BF16)
            leave = column(cols_ref, rows, lane)
            key_grad_ref[rows, cut] = (
                key_part_ref[rows, cut] + mm(value_ref[rows, cut], low, NT) * leave
            ).astype(BF16)
            value_grad_ref[rows, cut] = (
                value_part_ref[rows, cut] + mm(key_ref[rows, cut], low) * leave
            ).astype(BF16)


def rows_of(ref, j):
    return ref[j * DH : (j + 1) * DH, :]


def joined(later, got_ref, held_ref, heads, j):
    a_got = got_ref[heads * DH + j : heads * DH + j + 1, :]
    a_held = held_ref[heads * DH + j : heads * DH + j + 1, :]
    state = jnp.where(later, a_held, 1.0) * rows_of(got_ref, j) + jnp.where(later, 1.0, a_got) * rows_of(held_ref, j)
    return state, a_got * a_held


def c1_body(heads, pos, own_ref, got_ref, keep_ref, send_ref):
    later = (pos[0] & 1) == 1
    k = heads // 2
    for out in (keep_ref, send_ref):
        out[k * DH :, :] = jnp.ones((8, DH), F32)
    for j in range(heads):
        out, at = (keep_ref, j) if j < k else (send_ref, j - k)
        state, a = joined(later, got_ref, own_ref, heads, j)
        out[at * DH : (at + 1) * DH, :] = state
        out[k * DH + at : k * DH + at + 1, :] = a


def c2_body(k, pos, own_ref, got_ref, total_ref):
    later = (pos[0] & 2) == 2
    total_ref[k * DH :, :] = jnp.ones((8, DH), F32)
    for j in range(k):
        state, a = joined(later, got_ref, own_ref, k, j)
        total_ref[j * DH : (j + 1) * DH, :] = state
        total_ref[k * DH + j : k * DH + j + 1, :] = a


def before(later, got_ref, prefix_ref, k, j):
    a_got = got_ref[k * DH + j : k * DH + j + 1, :]
    if prefix_ref is None:
        return jnp.where(later, 1.0, 0.0) * rows_of(got_ref, j), jnp.where(later, a_got, 1.0)
    a = prefix_ref[k * DH + j : k * DH + j + 1, :]
    state = jnp.where(later, a, 0.0) * rows_of(got_ref, j) + rows_of(prefix_ref, j)
    return state, jnp.where(later, a * a_got, a)


def cz_body(k, bit, first, pos, *refs):
    if first:
        total_ref, got_ref, new_total_ref, new_prefix_ref = refs
        prefix_ref = None
    else:
        total_ref, got_ref, prefix_ref, new_total_ref, new_prefix_ref = refs
    later = (pos[0] & bit) == bit
    for out in (new_total_ref, new_prefix_ref):
        out[k * DH :, :] = jnp.ones((8, DH), F32)
    for j in range(k):
        at, one = slice(j * DH, (j + 1) * DH), slice(k * DH + j, k * DH + j + 1)
        new_total_ref[at, :], new_total_ref[one, :] = joined(later, got_ref, total_ref, k, j)
        new_prefix_ref[at, :], new_prefix_ref[one, :] = before(later, got_ref, prefix_ref, k, j)


def c3_body(k, bit, first, pos, *refs):
    if first:
        got_ref, own_ref, chip_ref, mine_ref, send_ref = refs
        prefix_ref = None
    else:
        got_ref, prefix_ref, own_ref, chip_ref, mine_ref, send_ref = refs
    later = (pos[0] & bit) == bit
    upper = (pos[0] & 2) == 2
    for j in range(k):
        at, one = slice(j * DH, (j + 1) * DH), slice(k * DH + j, k * DH + j + 1)
        prefix, _ = before(later, got_ref, prefix_ref, k, j)
        chip_a, chip = chip_ref[one, :], rows_of(chip_ref, j)
        own_a, own = own_ref[one, :], rows_of(own_ref, j)
        mine_ref[at, :] = jnp.where(upper, chip_a, 1.0) * prefix + jnp.where(upper, 1.0, 0.0) * chip
        send_ref[at, :] = jnp.where(upper, 1.0, own_a) * prefix + jnp.where(upper, 0.0, 1.0) * own


def c4_body(k, pos, half_ref, got_half_ref, own_ref, got_ref, mine_ref, send_ref):
    later = (pos[0] & 1) == 1
    heads = 2 * k
    for j in range(heads):
        at, one = slice(j * DH, (j + 1) * DH), slice(heads * DH + j, heads * DH + j + 1)
        chip = rows_of(half_ref, j) if j < k else rows_of(got_half_ref, j - k)
        mine_ref[at, :] = jnp.where(later, got_ref[one, :], 1.0) * chip + jnp.where(later, 1.0, 0.0) * rows_of(got_ref, j)
        send_ref[at, :] = jnp.where(later, 1.0, own_ref[one, :]) * chip + jnp.where(later, 0.0, 1.0) * rows_of(own_ref, j)


def small(body, pos, arrays, rows):
    return pl.pallas_call(
        body,
        in_specs=[pl.BlockSpec(memory_space=pltpu.SMEM)] + [pl.BlockSpec(memory_space=pltpu.VMEM)] * len(arrays),
        out_specs=[pl.BlockSpec(memory_space=pltpu.VMEM)] * len(rows),
        out_shape=[jax.ShapeDtypeStruct((r, DH), F32) for r in rows],
    )(pos, *arrays)


def exchange(x, bit, count):
    return lax.ppermute(x, "seq", [(i, i ^ bit) for i in range(count)])


def scan_devices(own, send, pos, k, count):
    full, half = 2 * k * DH + 8, k * DH + 8
    got = exchange(send, 1, count)
    chip, chip_send = small(functools.partial(c1_body, 2 * k), pos, (own, got), (half, half))
    chip_got = exchange(chip_send, 2, count)
    (total,) = small(functools.partial(c2_body, k), pos, (chip, chip_got), (half,))
    prefix = None
    bit = 4
    while bit < count:
        got_total = exchange(total, bit, count)
        held = () if prefix is None else (prefix,)
        if bit * 2 < count:
            total, prefix = small(
                functools.partial(cz_body, k, bit, prefix is None), pos, (total, got_total) + held, (half, half)
            )
        else:
            mine, mine_send = small(
                functools.partial(c3_body, k, bit, prefix is None),
                pos,
                (got_total,) + held + (chip, chip_got),
                (k * DH, k * DH),
            )
        bit *= 2
    mine_got = exchange(mine_send, 2, count)
    state, state_send = small(
        functools.partial(c4_body, k), pos, (mine, mine_got, own, got), (2 * k * DH, 2 * k * DH)
    )
    return state, exchange(state_send, 1, count)


def local(query_rows, key_rows, value_rows, log_decay, run_start, out_grad):
    heads = log_decay.shape[0]
    tokens, width = query_rows.shape
    count = lax.axis_size("seq")
    place = lax.axis_index("seq")
    k = heads // 4
    info = (((place & 1) << 1) | ((place >> 1) & 1)).reshape(1)
    forward_pos = place.reshape(1)
    backward_pos = (count - 1 - place).reshape(1)
    full = 2 * k * DH + 8

    grouped = pl.BlockSpec((tokens, k * DH), lambda g, q: (0, g ^ q[0]))
    grouped_state = pl.BlockSpec((k, DH, DH), lambda g, q: (g ^ q[0], 0, 0))
    grouped_low = pl.BlockSpec((k, 2, DH, DH), lambda g, q: (g ^ q[0], 0, 0, 0))
    by_head = pl.BlockSpec((tokens, DH), lambda h: (0, h))
    rows_spec, cols_spec = whole((32, tokens)), whole((tokens, DH))
    message = jax.ShapeDtypeStruct((full, DH), F32)
    states_f32 = jax.ShapeDtypeStruct((heads, DH, DH), F32)
    flat_bf16 = jax.ShapeDtypeStruct((tokens, width), BF16)
    flat_f32 = jax.ShapeDtypeStruct((tokens, width), F32)

    own, send, loc, rows, cols = pl.pallas_call(
        functools.partial(k1_body, k),
        grid_spec=pltpu.PrefetchScalarGridSpec(
            num_scalar_prefetch=1,
            grid=(4,),
            in_specs=[grouped, grouped, whole((heads, tokens)), whole((1, tokens))],
            out_specs=[whole((full, DH)), whole((full, DH)), grouped_state, rows_spec, cols_spec],
        ),
        out_shape=[
            message,
            message,
            states_f32,
            jax.ShapeDtypeStruct((32, tokens), F32),
            jax.ShapeDtypeStruct((tokens, DH), F32),
        ],
    )(info, key_rows, value_rows, log_decay, run_start.reshape(1, tokens))

    mine, other = scan_devices(own, send, forward_pos, k, count)

    weighted_spec = pl.BlockSpec((None, 2, BLOCK, BLOCK), lambda h: (h, 0, 0, 0))
    within, weighted = pl.pallas_call(
        k2_body,
        grid=(heads,),
        in_specs=[by_head, by_head, by_head, rows_spec, cols_spec],
        out_specs=[by_head, weighted_spec],
        out_shape=[flat_f32, jax.ShapeDtypeStruct((heads, 2, BLOCK, BLOCK), BF16)],
        cost_estimate=pl.CostEstimate(flops=800_000_000, bytes_accessed=8_000_000, transcendentals=1_000_000),
    )(query_rows, key_rows, value_rows, rows, cols)

    attended, mixgrad, states_low, own, send, back = pl.pallas_call(
        functools.partial(k3_body, k),
        grid_spec=pltpu.PrefetchScalarGridSpec(
            num_scalar_prefetch=1,
            grid=(4,),
            in_specs=[grouped, grouped, grouped, grouped_state, rows_spec, cols_spec]
            + [whole((2 * k * DH, DH))] * 2,
            out_specs=[grouped, grouped, grouped_low, whole((full, DH)), whole((full, DH)), grouped_state],
        ),
        out_shape=[
            flat_bf16,
            flat_bf16,
            jax.ShapeDtypeStruct((heads, 2, DH, DH), BF16),
            message,
            message,
            states_f32,
        ],
    )(info, query_rows, out_grad, within, loc, rows, cols, mine, other)

    mine, other = scan_devices(own, send, backward_pos, k, count)

    query_grad, key_part, value_part = pl.pallas_call(
        k4_body,
        grid=(heads,),
        in_specs=[
            by_head,
            by_head,
            by_head,
            by_head,
            weighted_spec,
            pl.BlockSpec((1, 2, DH, DH), lambda h: (h, 0, 0, 0)),
            rows_spec,
            cols_spec,
        ],
        out_specs=[by_head, by_head, by_head],
        out_shape=[flat_bf16, flat_f32, flat_f32],
        cost_estimate=pl.CostEstimate(flops=1_600_000_000, bytes_accessed=12_000_000, transcendentals=1_000_000),
    )(query_rows, key_rows, value_rows, mixgrad, weighted, states_low, rows, cols)

    key_grad, value_grad = pl.pallas_call(
        functools.partial(k5_body, k),
        grid_spec=pltpu.PrefetchScalarGridSpec(
            num_scalar_prefetch=1,
            grid=(4,),
            in_specs=[grouped] * 4 + [grouped_state, rows_spec, cols_spec] + [whole((2 * k * DH, DH))] * 2,
            out_specs=[grouped, grouped],
        ),
        out_shape=[flat_bf16, flat_bf16],
    )(info, key_rows, value_rows, key_part, value_part, back, rows, cols, mine, other)
    return attended, query_grad, key_grad, value_grad


def solution(mesh):
    rows = P(("groups", "seq"), None)
    return jax.shard_map(
        local,
        mesh=mesh,
        in_specs=(rows, rows, rows, P(None, ("groups", "seq")), P(("groups", "seq")), rows),
        out_specs=(rows, rows, rows, rows),
        check_vma=False,
    )
```

```python
import functools

import jax
import jax.numpy as jnp
from jax import lax
from jax.experimental import pallas as pl
from jax.experimental.pallas import tpu as pltpu
from jax.sharding import PartitionSpec as P

BLOCK = 256
HALF = 128
DH = 128
EPS = 1e-05
FAR = -1e30
GROUPS = 4
CHUNKS = 1
PIECES = 4
F32 = jnp.float32
BF16 = jnp.bfloat16

NN = (((1,), (0,)), ((), ()))
NT = (((1,), (1,)), ((), ()))
TN = (((0,), (0,)), ((), ()))


def mm(a, b, dims=NN):
    return lax.dot_general(a, b, dims, preferred_element_type=F32)


def cut(j):
    return slice(j * DH, (j + 1) * DH)


def block(b):
    return slice(b * BLOCK, (b + 1) * BLOCK)


SMEM = pl.BlockSpec(memory_space=pltpu.SMEM)
VMEM = pl.BlockSpec(memory_space=pltpu.VMEM)
ANY = pl.BlockSpec(memory_space=pl.ANY)


def run(body, scalar, inside, outs, outside=(), after=(), aliases=None, scratch=(), megabytes=8):
    taken = len(inside) + len(outside)

    def kernel(scalar_ref, *refs):
        body(scalar_ref, *refs[:taken], *refs[taken + len(after) :])

    shapes = [o if isinstance(o, jax.ShapeDtypeStruct) else pltpu.VMEM(*o) for o in outs]
    return pl.pallas_call(
        kernel,
        in_specs=[SMEM] + [VMEM] * len(inside) + [ANY] * (len(outside) + len(after)),
        out_specs=[ANY if isinstance(o, jax.ShapeDtypeStruct) else VMEM for o in outs],
        out_shape=shapes,
        input_output_aliases={1 + len(inside) + i: o for i, o in (aliases or {}).items()},
        scratch_shapes=list(scratch),
        compiler_params=pltpu.CompilerParams(vmem_limit_bytes=megabytes << 20),
    )(scalar, *[pltpu.with_memory_space_constraint(a, pltpu.VMEM) for a in inside], *outside, *after)


def prepare(decay_ref, start_ref, rows_ref, cols_ref):
    tri = (
        lax.broadcasted_iota(jnp.int32, (BLOCK, BLOCK), 0) <= lax.broadcasted_iota(jnp.int32, (BLOCK, BLOCK), 1)
    ).astype(F32)
    for b in range(decay_ref.shape[1] // BLOCK):
        at = block(b)
        starts = jnp.broadcast_to(start_ref[:, at].astype(F32), (8, BLOCK))
        both = jnp.concatenate([decay_ref[:, at], starts], axis=0)
        sums = lax.dot_general(both, tri, NN, precision=lax.Precision.HIGHEST, preferred_element_type=F32)
        cumul, marks = sums[:8], sums[8:]
        last, last_mark = cumul[:, BLOCK - 1 :], marks[:, BLOCK - 1 :]
        entering = jnp.where(marks == 0.0, jnp.exp(cumul), 0.0)
        leaving = jnp.where(marks == last_mark, jnp.exp(last - cumul), 0.0)
        stack = jnp.concatenate([cumul, entering, leaving, marks], axis=0)
        rows_ref[:, at] = stack
        cols_ref[at, :] = jnp.concatenate([stack, jnp.zeros((96, BLOCK), F32)], axis=0).T


def keeps(rows_ref, head):
    enter = rows_ref[8 + head : 9 + head, :]
    k0 = jnp.broadcast_to(enter[:, BLOCK - 1 : BLOCK], (1, DH))
    k1 = jnp.broadcast_to(enter[:, 2 * BLOCK - 1 : 2 * BLOCK], (1, DH))
    return k0, k1


def send_out(info, k, terms_ref, keep_ref, own_ref, send_ref):
    for out, first in ((own_ref, 0), (send_ref, 2 * k)):
        for r in range(2 * k):
            group, j = (first + r) // k, (first + r) % k
            head = (group ^ info[0]) * k + j
            out[cut(r), :] = terms_ref[head]
            out[pl.ds(2 * k * DH + r, 1), :] = keep_ref[pl.ds(head, 1), :]
        rest = 8 - 2 * k
        out[2 * k * DH + 2 * k :, :] = jnp.ones((rest, DH), F32)


def k1_body(k, head0, info, decay_ref, start_ref, key_hbm, value_hbm,
            own_ref, send_ref, loc_ref, rows_ref, cols_ref, key_ref, value_ref, terms_ref, keep_ref, sems):
    heads = GROUPS * k
    copies = []
    for j in range(heads):
        pair = []
        for i, (source, target) in enumerate(((key_hbm, key_ref), (value_hbm, value_ref))):
            copy = pltpu.make_async_copy(source.at[:, cut(head0 + j)], target.at[:, cut(j)], sems.at[2 * j + i])
            copy.start()
            pair.append(copy)
        copies.append(pair)
    prepare(decay_ref, start_ref, rows_ref, cols_ref)
    for j in range(heads):
        for copy in copies[j]:
            copy.wait()
        head = head0 + j
        leave = rows_ref[16 + head : 17 + head, :]
        terms = []
        for b in range(2):
            keys = key_ref[block(b), cut(j)].T.astype(F32)
            scaled = (keys * leave[:, block(b)]).astype(BF16)
            terms.append(mm(scaled, value_ref[block(b), cut(j)]))
        k0, k1 = keeps(rows_ref, head)
        loc_ref[j] = terms[0]
        terms_ref[j] = k1 * terms[0] + terms[1]
        keep_ref[j : j + 1, :] = k0 * k1
    send_out(info, k, terms_ref, keep_ref, own_ref, send_ref)


def make_bias(cols_ref, rows_ref, bias_ref):
    lower = lax.broadcasted_iota(jnp.int32, (BLOCK, BLOCK), 0) >= lax.broadcasted_iota(jnp.int32, (BLOCK, BLOCK), 1)
    for b in range(2):
        same = cols_ref[block(b), 24:25] == rows_ref[24:25, block(b)]
        bias_ref[b] = jnp.where(lower & same, 0.0, FAR)


def k2_body(first, head0, base, count, info, query_ref, key_ref, value_ref, rows_ref, cols_ref, *refs):
    if first:
        within_ref, weighted_ref, grid_ref, scaled_ref, bias_ref = refs
        make_bias(cols_ref, rows_ref, bias_ref)
    else:
        bias_ref, within_ref, weighted_ref, grid_ref, scaled_ref = refs
    for j in range(count):
        head = head0 + j
        inner = head - base
        for b in range(2):
            at = block(b)
            query = query_ref[at, cut(head)]
            scores = mm(query, key_ref[at, cut(inner)], NT)
            cum_row = rows_ref[head : head + 1, at]
            for part, width in ((0, HALF), (1, BLOCK)):
                up = slice(part * HALF, (part + 1) * HALF)
                cum_col = cols_ref[b * BLOCK + part * HALF : b * BLOCK + (part + 1) * HALF, head : head + 1]
                grid = jnp.exp(jnp.minimum(cum_col - cum_row[:, :width], bias_ref[b, up, :width]))
                grid_ref[j, b, up, :width] = grid
                weighted_ref[j, b, up, :width] = (scores[up, :width] * grid).astype(BF16)
            grid_ref[j, b, :HALF, HALF:] = jnp.zeros((HALF, HALF), F32)
            weighted_ref[j, b, :HALF, HALF:] = jnp.zeros((HALF, HALF), BF16)
            within_ref[at, cut(j)] = mm(weighted_ref[j, b], value_ref[at, cut(inner)])
            enter = rows_ref[8 + head : 9 + head, at]
            scaled_ref[j, b] = (query.T.astype(F32) * enter).astype(BF16)


def k3_body(k, head0, pieces, per, has_alias, info, query_ref, grad_ref, loc_ref, rows_ref, cols_ref, mine_ref,
            other_ref, *refs):
    withins, scaleds = refs[:pieces], refs[pieces : 2 * pieces]
    refs = refs[2 * pieces + has_alias :]
    own_ref, send_ref, mixgrad_ref, states_ref, back_ref, attended_hbm = refs[:6]
    attended_ref, terms_ref, keep_ref, state_ref, sems = refs[6:]
    heads = GROUPS * k
    for r in range(heads):
        group, j = r // k, r % k
        source = mine_ref if r < 2 * k else other_ref
        state_ref[(group ^ info[0]) * k + j] = source[cut(r % (2 * k)), :]
    copies = []
    for j in range(heads):
        head = head0 + j
        within_ref, scaled_ref, i = withins[j // per], scaleds[j // per], j % per
        k0, k1 = keeps(rows_ref, head)
        incoming = state_ref[j]
        states = (incoming, k0 * incoming + loc_ref[j])
        backs = []
        for b in range(2):
            at = block(b)
            low = states[b].astype(BF16)
            states_ref[j, b] = low
            enter = cols_ref[at, 8 + head : 9 + head]
            mixture = within_ref[at, cut(i)] + mm(query_ref[at, cut(head)], low) * enter
            inverse = lax.rsqrt(jnp.mean(mixture * mixture, axis=1, keepdims=True) + EPS)
            normed = mixture * inverse
            attended_ref[at, cut(j)] = normed.astype(BF16)
            wide = grad_ref[at, cut(head)].astype(F32)
            mixgrad = (inverse * (wide - normed * jnp.mean(wide * normed, axis=1, keepdims=True))).astype(BF16)
            mixgrad_ref[at, cut(j)] = mixgrad
            backs.append(mm(scaled_ref[i, b], mixgrad))
        copy = pltpu.make_async_copy(attended_ref.at[:, cut(j)], attended_hbm.at[:, cut(head)], sems.at[j])
        copy.start()
        copies.append(copy)
        back_ref[j] = backs[1]
        terms_ref[j] = k0 * backs[1] + backs[0]
        keep_ref[j : j + 1, :] = k0 * k1
    send_out(info, k, terms_ref, keep_ref, own_ref, send_ref)
    for copy in copies:
        copy.wait()


def k4_body(head0, base, count, has_alias, info, query_ref, key_ref, value_ref, mixgrad_ref, weighted_ref, grid_ref,
            states_ref, cols_ref, *refs):
    key_part_ref, value_part_ref, query_grad_hbm, query_grad_ref, sems = refs[has_alias:]
    copies = []
    for j in range(count):
        head = head0 + j
        inner = head - base
        for b in range(2):
            at = block(b)
            mixgrad = mixgrad_ref[at, cut(inner)]
            masked = (mm(mixgrad, value_ref[at, cut(inner)], NT) * grid_ref[j, b]).astype(BF16)
            enter = cols_ref[at, 8 + head : 9 + head]
            query_grad_ref[at, cut(j)] = (
                mm(masked, key_ref[at, cut(inner)]) + mm(mixgrad, states_ref[inner, b], NT) * enter
            ).astype(BF16)
            key_part_ref[at, cut(j)] = mm(masked, query_ref[at, cut(head)], TN)
            value_part_ref[at, cut(j)] = mm(weighted_ref[j, b], mixgrad, TN)
        copy = pltpu.make_async_copy(query_grad_ref.at[:, cut(j)], query_grad_hbm.at[:, cut(head)], sems.at[j])
        copy.start()
        copies.append(copy)
    for copy in copies:
        copy.wait()


def k5_body(k, head0, pieces, per, has_alias, info, key_ref, value_ref, back_ref, rows_ref, cols_ref, mine_ref,
            other_ref, *refs):
    key_parts, value_parts = refs[:pieces], refs[pieces : 2 * pieces]
    refs = refs[2 * pieces + 2 * has_alias :]
    key_grad_hbm, value_grad_hbm, key_grad_ref, value_grad_ref, state_ref, sems = refs
    heads = GROUPS * k
    for r in range(heads):
        group, j = r // k, r % k
        source = mine_ref if r < 2 * k else other_ref
        state_ref[(group ^ info[0]) * k + j] = source[cut(r % (2 * k)), :]
    copies = []
    for j in range(heads):
        head = head0 + j
        i = j % per
        k0, k1 = keeps(rows_ref, head)
        outgoing = state_ref[j]
        afters = (k1 * outgoing + back_ref[j], outgoing)
        for b in range(2):
            at = block(b)
            low = afters[b].astype(BF16)
            leave = cols_ref[at, 16 + head : 17 + head]
            key_grad_ref[at, cut(j)] = (
                key_parts[j // per][at, cut(i)] + mm(value_ref[at, cut(j)], low, NT) * leave
            ).astype(BF16)
            value_grad_ref[at, cut(j)] = (
                value_parts[j // per][at, cut(i)] + mm(key_ref[at, cut(j)], low) * leave
            ).astype(BF16)
        for n, (source, target) in enumerate(((key_grad_ref, key_grad_hbm), (value_grad_ref, value_grad_hbm))):
            copy = pltpu.make_async_copy(source.at[:, cut(j)], target.at[:, cut(head)], sems.at[2 * j + n])
            copy.start()
            copies.append(copy)
    for copy in copies:
        copy.wait()


def joined(later, got_ref, held_ref, heads, j):
    one = slice(heads * DH + j, heads * DH + j + 1)
    a_got, a_held = got_ref[one, :], held_ref[one, :]
    state = jnp.where(later, a_held, 1.0) * got_ref[cut(j), :] + jnp.where(later, 1.0, a_got) * held_ref[cut(j), :]
    return state, a_got * a_held


def before(later, got_ref, prefix_ref, k, j):
    one = slice(k * DH + j, k * DH + j + 1)
    a_got = got_ref[one, :]
    if prefix_ref is None:
        return jnp.where(later, 1.0, 0.0) * got_ref[cut(j), :], jnp.where(later, a_got, 1.0)
    a = prefix_ref[one, :]
    state = jnp.where(later, a, 0.0) * got_ref[cut(j), :] + prefix_ref[cut(j), :]
    return state, jnp.where(later, a * a_got, a)


def put(out, heads, j, value):
    out[cut(j), :], out[heads * DH + j : heads * DH + j + 1, :] = value


def c1_body(k, pos, own_ref, got_ref, keep_ref, send_ref):
    later = (pos[0] & 1) == 1
    for out in (keep_ref, send_ref):
        out[k * DH :, :] = jnp.ones((8, DH), F32)
    for j in range(2 * k):
        put(keep_ref if j < k else send_ref, k, j % k, joined(later, got_ref, own_ref, 2 * k, j))


def c2_body(k, pos, own_ref, got_ref, total_ref):
    later = (pos[0] & 2) == 2
    total_ref[k * DH :, :] = jnp.ones((8, DH), F32)
    for j in range(k):
        put(total_ref, k, j, joined(later, got_ref, own_ref, k, j))


def cz_body(k, bit, first, pos, *refs):
    total_ref, got_ref = refs[:2]
    prefix_ref = None if first else refs[2]
    new_total_ref, new_prefix_ref = refs[-2:]
    later = (pos[0] & bit) == bit
    for out in (new_total_ref, new_prefix_ref):
        out[k * DH :, :] = jnp.ones((8, DH), F32)
    for j in range(k):
        put(new_total_ref, k, j, joined(later, got_ref, total_ref, k, j))
        put(new_prefix_ref, k, j, before(later, got_ref, prefix_ref, k, j))


def c3_body(k, bit, first, pos, *refs):
    got_ref = refs[0]
    prefix_ref = None if first else refs[1]
    own_ref, chip_ref, mine_ref, send_ref = refs[-4:]
    later = (pos[0] & bit) == bit
    upper = (pos[0] & 2) == 2
    for j in range(k):
        at, one = cut(j), slice(k * DH + j, k * DH + j + 1)
        prefix, _ = before(later, got_ref, prefix_ref, k, j)
        mine_ref[at, :] = jnp.where(upper, chip_ref[one, :], 1.0) * prefix + jnp.where(upper, 1.0, 0.0) * chip_ref[at, :]
        send_ref[at, :] = jnp.where(upper, 1.0, own_ref[one, :]) * prefix + jnp.where(upper, 0.0, 1.0) * own_ref[at, :]


def c4_body(k, pos, half_ref, got_half_ref, own_ref, got_ref, mine_ref, send_ref):
    later = (pos[0] & 1) == 1
    for j in range(2 * k):
        at, one = cut(j), slice(2 * k * DH + j, 2 * k * DH + j + 1)
        chip = half_ref[cut(j), :] if j < k else got_half_ref[cut(j - k), :]
        mine_ref[at, :] = jnp.where(later, got_ref[one, :], 1.0) * chip + jnp.where(later, 1.0, 0.0) * got_ref[at, :]
        send_ref[at, :] = jnp.where(later, 1.0, own_ref[one, :]) * chip + jnp.where(later, 0.0, 1.0) * own_ref[at, :]


def exchange(x, bit, count):
    return lax.ppermute(x, "seq", [(i, i ^ bit) for i in range(count)])


def scan_devices(own, send, pos, k, count, fillers):
    half = ((k * DH + 8, DH), F32)
    got = exchange(send, 1, count)
    yield send
    chip, chip_send = run(functools.partial(c1_body, k), pos, (own, got), (half, half))
    chip_got = exchange(chip_send, 2, count)
    filled = yield chip_send
    (total,) = run(functools.partial(c2_body, k), pos, (chip, chip_got), (half,), after=filled)
    prefix = ()
    bit = 4
    while bit < count:
        got_total = exchange(total, bit, count)
        filled = yield total
        if bit * 2 < count:
            body = functools.partial(cz_body, k, bit, not prefix)
            total, *prefix = run(body, pos, (total, got_total, *prefix), (half, half), after=filled)
        else:
            body = functools.partial(c3_body, k, bit, not prefix)
            outs = (((k * DH, DH), F32),) * 2
            mine, mine_send = run(body, pos, (got_total, *prefix, chip, chip_got), outs, after=filled)
        bit *= 2
    mine_got = exchange(mine_send, 2, count)
    filled = yield mine_send
    outs = (((2 * k * DH, DH), F32),) * 2
    state, state_send = run(
        functools.partial(c4_body, k), pos, (mine, mine_got, own, got), outs, after=filled
    )
    yield state, exchange(state_send, 1, count)


def drive(scan, fillers):
    out = next(scan)
    fillers = list(fillers)
    out = next(scan)
    while not isinstance(out, tuple):
        done = ()
        if fillers:
            done = tuple(fillers.pop(0)(out))
        out = scan.send(done)
    for filler in fillers:
        filler(None)
    return out


def local(query_rows, key_rows, value_rows, log_decay, run_start, out_grad):
    all_heads = log_decay.shape[0]
    tokens, width = query_rows.shape
    count = lax.axis_size("seq")
    place = lax.axis_index("seq")
    info = (((place & 1) << 1) | ((place >> 1) & 1)).reshape(1)
    forward_pos = place.reshape(1)
    backward_pos = (count - 1 - place).reshape(1)
    k = all_heads // GROUPS
    heads = all_heads
    per = heads // PIECES
    dma = pltpu.SemaphoreType.DMA
    message = ((2 * k * DH + 8, DH), F32)
    states = ((heads, DH, DH), F32)
    flat = jax.ShapeDtypeStruct((tokens, width), BF16)
    chunk_bf16 = ((tokens, heads * DH), BF16)
    piece_f32 = ((tokens, per * DH), F32)
    scratch_terms = (pltpu.VMEM((heads, DH, DH), F32), pltpu.VMEM((8, DH), F32))

    own, send, loc, rows, cols, keys, values = run(
        functools.partial(k1_body, k, 0),
        info,
        (log_decay, run_start.reshape(1, tokens)),
        (message, message, states, ((32, tokens), F32), ((tokens, DH), F32), chunk_bf16, chunk_bf16),
        outside=(key_rows, value_rows),
        scratch=scratch_terms + (dma((2 * heads,)),),
    )

    forward = []

    def k2(p, sent):
        grids = ((per, 2, BLOCK, BLOCK), F32)
        outs = (piece_f32, ((per, 2, BLOCK, BLOCK), BF16), grids, ((per, 2, DH, BLOCK), BF16))
        inputs = (query_rows, keys, values, rows, cols)
        if p == 0:
            outs += (((2, BLOCK, BLOCK), F32),)
        else:
            inputs += (forward[0][4],)
        result = run(
            functools.partial(k2_body, p == 0, p * per, 0, per),
            info, inputs, outs, after=() if sent is None else (sent,),
        )
        forward.append(result)
        return result[:1]

    mine, other = drive(
        scan_devices(own, send, forward_pos, k, count, None), [functools.partial(k2, p) for p in range(PIECES)]
    )
    own, send, mixgrad, states_low, back, attended = run(
        functools.partial(k3_body, k, 0, PIECES, per, 0),
        info,
        (query_rows, out_grad, loc, rows, cols, mine, other, *[f[0] for f in forward], *[f[3] for f in forward]),
        (message, message, chunk_bf16, ((heads, 2, DH, DH), BF16), states, flat),
        scratch=(pltpu.VMEM((tokens, heads * DH), BF16),) + scratch_terms
        + (pltpu.VMEM((heads, DH, DH), F32), dma((heads,))),
    )

    backward = []

    def k4(p, sent):
        has_alias = int(bool(backward))
        result = run(
            functools.partial(k4_body, p * per, 0, per, has_alias),
            info,
            (query_rows, keys, values, mixgrad, forward[p][1], forward[p][2], states_low, cols),
            (piece_f32, piece_f32, flat),
            outside=(backward[-1][2],) if backward else (),
            after=() if sent is None else (sent,),
            aliases={0: 2} if backward else None,
            scratch=(pltpu.VMEM((tokens, per * DH), BF16), dma((per,))),
        )
        backward.append(result)
        return result[:1]

    mine, other = drive(
        scan_devices(own, send, backward_pos, k, count, None), [functools.partial(k4, p) for p in range(PIECES)]
    )
    key_grad, value_grad = run(
        functools.partial(k5_body, k, 0, PIECES, per, 0),
        info,
        (keys, values, back, rows, cols, mine, other, *[b[0] for b in backward], *[b[1] for b in backward]),
        (flat, flat),
        scratch=(pltpu.VMEM((tokens, heads * DH), BF16),) * 2
        + (pltpu.VMEM((heads, DH, DH), F32), dma((2 * heads,))),
    )
    return attended, backward[-1][2], key_grad, value_grad


def solution(mesh):
    rows = P(("groups", "seq"), None)
    return jax.shard_map(
        local,
        mesh=mesh,
        in_specs=(rows, rows, rows, P(None, ("groups", "seq")), P(("groups", "seq")), rows),
        out_specs=(rows, rows, rows, rows),
        check_vma=False,
    )
```

```python
import functools

import jax
import jax.numpy as jnp
from jax import lax
from jax.experimental import pallas as pl
from jax.experimental.pallas import tpu as pltpu
from jax.sharding import PartitionSpec as P

BLOCK = 256
HALF = 128
DH = 128
EPS = 1e-05
FAR = -1e30
GROUPS = 4
CHUNKS = 2
PIECES = 2
F32 = jnp.float32
BF16 = jnp.bfloat16

NN = (((1,), (0,)), ((), ()))
NT = (((1,), (1,)), ((), ()))
TN = (((0,), (0,)), ((), ()))


def mm(a, b, dims=NN):
    return lax.dot_general(a, b, dims, preferred_element_type=F32)


def cut(j):
    return slice(j * DH, (j + 1) * DH)


def block(b):
    return slice(b * BLOCK, (b + 1) * BLOCK)


SMEM = pl.BlockSpec(memory_space=pltpu.SMEM)
VMEM = pl.BlockSpec(memory_space=pltpu.VMEM)
ANY = pl.BlockSpec(memory_space=pl.ANY)
HBM = pl.BlockSpec(memory_space=pltpu.HBM)


def run(body, scalar, inside, outs, outside=(), after=(), aliases=None, scratch=(), megabytes=8):
    taken = len(inside) + len(outside)

    def kernel(scalar_ref, *refs):
        body(scalar_ref, *refs[:taken], *refs[taken + len(after) :])

    shapes = [pltpu.HBM(o.shape, o.dtype) if isinstance(o, jax.ShapeDtypeStruct) else pltpu.VMEM(*o) for o in outs]
    return pl.pallas_call(
        kernel,
        in_specs=[SMEM] + [VMEM] * len(inside) + [HBM] * len(outside) + [ANY] * len(after),
        out_specs=[HBM if isinstance(o, jax.ShapeDtypeStruct) else VMEM for o in outs],
        out_shape=shapes,
        input_output_aliases={1 + len(inside) + i: o for i, o in (aliases or {}).items()},
        scratch_shapes=list(scratch),
        compiler_params=pltpu.CompilerParams(vmem_limit_bytes=megabytes << 20),
    )(scalar, *[pltpu.with_memory_space_constraint(a, pltpu.VMEM) for a in inside],
      *[pltpu.with_memory_space_constraint(a, pltpu.HBM) for a in outside], *after)


def prepare(decay_ref, start_ref, rows_ref, cols_ref):
    tri = (
        lax.broadcasted_iota(jnp.int32, (BLOCK, BLOCK), 0) <= lax.broadcasted_iota(jnp.int32, (BLOCK, BLOCK), 1)
    ).astype(F32)
    for b in range(decay_ref.shape[1] // BLOCK):
        at = block(b)
        starts = jnp.broadcast_to(start_ref[:, at].astype(F32), (8, BLOCK))
        both = jnp.concatenate([decay_ref[:, at], starts], axis=0)
        sums = lax.dot_general(both, tri, NN, precision=lax.Precision.HIGHEST, preferred_element_type=F32)
        cumul, marks = sums[:8], sums[8:]
        last, last_mark = cumul[:, BLOCK - 1 :], marks[:, BLOCK - 1 :]
        entering = jnp.where(marks == 0.0, jnp.exp(cumul), 0.0)
        leaving = jnp.where(marks == last_mark, jnp.exp(last - cumul), 0.0)
        stack = jnp.concatenate([cumul, entering, leaving, marks], axis=0)
        rows_ref[:, at] = stack
        cols_ref[at, :] = jnp.concatenate([stack, jnp.zeros((96, BLOCK), F32)], axis=0).T


def keeps(rows_ref, head):
    enter = rows_ref[8 + head : 9 + head, :]
    k0 = jnp.broadcast_to(enter[:, BLOCK - 1 : BLOCK], (1, DH))
    k1 = jnp.broadcast_to(enter[:, 2 * BLOCK - 1 : 2 * BLOCK], (1, DH))
    return k0, k1


def send_out(place, k, terms_ref, keep_ref, own_ref, send_ref):
    for out, first in ((own_ref, 0), (send_ref, 2 * k)):
        for r in range(2 * k):
            group, j = (first + r) // k, (first + r) % k
            head = (group ^ place[0]) * k + j
            out[cut(r), :] = terms_ref[head]
            out[pl.ds(2 * k * DH + r, 1), :] = keep_ref[pl.ds(head, 1), :]
        rest = 8 - 2 * k
        out[2 * k * DH + 2 * k :, :] = jnp.ones((rest, DH), F32)


def take_in(place, k, mine_ref, other_ref, state_ref):
    for r in range(GROUPS * k):
        source = mine_ref if r < 2 * k else other_ref
        state_ref[((r // k) ^ place[0]) * k + r % k] = source[cut(r % (2 * k)), :]


def k1_body(k, head0, place, *refs):
    heads = GROUPS * k
    loads = []
    if head0 == 0:
        (decay_hbm, start_hbm, key_hbm, value_hbm, own_ref, send_ref, loc_ref, key_ref, value_ref, rows_ref, cols_ref,
         terms_ref, keep_ref, sems, decay_ref, start_ref) = refs
        loads = [
            pltpu.make_async_copy(decay_hbm, decay_ref, sems.at[2 * heads]),
            pltpu.make_async_copy(start_hbm, start_ref, sems.at[2 * heads + 1]),
        ]
    else:
        (rows_ref, key_hbm, value_hbm, own_ref, send_ref, loc_ref, key_ref, value_ref,
         terms_ref, keep_ref, sems) = refs
    for j in range(heads):
        for i, (source, target) in enumerate(((key_hbm, key_ref), (value_hbm, value_ref))):
            loads.append(
                pltpu.make_async_copy(source.at[:, cut(head0 + j)], target.at[:, cut(j)], sems.at[2 * j + i])
            )
    for load in loads:
        load.start()
    if head0 == 0:
        loads[0].wait()
        loads[1].wait()
        prepare(decay_ref, start_ref, rows_ref, cols_ref)
    for load in loads[-2 * heads :]:
        load.wait()
    for j in range(heads):
        head = head0 + j
        leave = rows_ref[16 + head : 17 + head, :]
        terms = []
        for b in range(2):
            keys = key_ref[block(b), cut(j)].T.astype(F32)
            scaled = (keys * leave[:, block(b)]).astype(BF16)
            terms.append(mm(scaled, value_ref[block(b), cut(j)]))
        k0, k1 = keeps(rows_ref, head)
        loc_ref[j] = terms[0]
        terms_ref[j] = k1 * terms[0] + terms[1]
        keep_ref[j : j + 1, :] = k0 * k1
    send_out(place, k, terms_ref, keep_ref, own_ref, send_ref)


def make_bias(rows_ref, cols_ref, bias_ref, turned_ref):
    down = lax.broadcasted_iota(jnp.int32, (BLOCK, BLOCK), 0)
    along = lax.broadcasted_iota(jnp.int32, (BLOCK, BLOCK), 1)
    for b in range(2):
        same = cols_ref[block(b), 24:25] == rows_ref[24:25, block(b)]
        bias_ref[b] = jnp.where((down >= along) & same, 0.0, FAR)
        turned_ref[b] = jnp.where((down <= along) & same, 0.0, FAR)


def k2_body(first, head0, base, count, place, query_ref, key_ref, value_ref, rows_ref, cols_ref, *refs):
    if first:
        (within_ref, grid_ref, turned_ref, weighted_ref, scaled_ref, enter_ref, leave_ref,
         bias_ref, bias_turned_ref) = refs
        make_bias(rows_ref, cols_ref, bias_ref, bias_turned_ref)
    else:
        (bias_ref, bias_turned_ref, within_ref, grid_ref, turned_ref, weighted_ref, scaled_ref, enter_ref,
         leave_ref) = refs
    zeros = jnp.zeros((HALF, HALF), F32)
    for j in range(count):
        head = head0 + j
        inner = head - base
        for b in range(2):
            at = block(b)
            query, key = query_ref[at, cut(head)], key_ref[at, cut(inner)]
            cum_row = rows_ref[head : head + 1, at]
            top, low = slice(0, HALF), slice(HALF, BLOCK)
            cum_top = jnp.broadcast_to(cols_ref[b * BLOCK : b * BLOCK + HALF, head : head + 1], (HALF, HALF))
            cum_low = jnp.broadcast_to(cols_ref[b * BLOCK + HALF : (b + 1) * BLOCK, head : head + 1], (HALF, HALF))
            row_top, row_low = cum_row[:, :HALF], cum_row[:, HALF:]

            def decay(difference, limit):
                return jnp.exp(jnp.minimum(difference, limit))

            grid_ref[j, b, top, top] = decay(cum_top - row_top, bias_ref[b, top, top])
            grid_ref[j, b, low, top] = decay(cum_low - row_top, bias_ref[b, low, top])
            grid_ref[j, b, low, low] = decay(cum_low - row_low, bias_ref[b, low, low])
            grid_ref[j, b, top, low] = zeros
            turned_ref[j, b, top, top] = decay(row_top - cum_top, bias_turned_ref[b, top, top])
            turned_ref[j, b, top, low] = decay(row_low - cum_top, bias_turned_ref[b, top, low])
            turned_ref[j, b, low, low] = decay(row_low - cum_low, bias_turned_ref[b, low, low])
            turned_ref[j, b, low, top] = zeros
            weighted = (mm(query, key, NT) * grid_ref[j, b]).astype(BF16)
            weighted_ref[j, b] = (mm(key, query, NT) * turned_ref[j, b]).astype(BF16)
            within_ref[at, cut(j)] = mm(weighted, value_ref[at, cut(inner)])
            enter = rows_ref[8 + head : 9 + head, at]
            scaled_ref[j, b] = (query.T.astype(F32) * enter).astype(BF16)
            enter_ref[at, cut(j)] = jnp.broadcast_to(cols_ref[at, 8 + head : 9 + head], (BLOCK, DH))
            leave_ref[at, cut(j)] = jnp.broadcast_to(cols_ref[at, 16 + head : 17 + head], (BLOCK, DH))


def k3_body(k, head0, pieces, per, place, query_ref, grad_ref, loc_ref, rows_ref, mine_ref, other_ref, *refs):
    withins, scaleds, enters = refs[:pieces], refs[pieces : 2 * pieces], refs[2 * pieces : 3 * pieces]
    own_ref, send_ref, mixgrad_ref, states_ref, back_ref, attended_ref = refs[3 * pieces : 3 * pieces + 6]
    terms_ref, keep_ref, state_ref = refs[3 * pieces + 6 :]
    take_in(place, k, mine_ref, other_ref, state_ref)
    for j in range(GROUPS * k):
        head = head0 + j
        p, i = j // per, j % per
        k0, k1 = keeps(rows_ref, head)
        incoming = state_ref[j]
        states = (incoming, k0 * incoming + loc_ref[j])
        backs = []
        for b in range(2):
            at = block(b)
            low = states[b].astype(BF16)
            states_ref[j, b] = low
            mixture = withins[p][at, cut(i)] + mm(query_ref[at, cut(head)], low) * enters[p][at, cut(i)]
            wide = grad_ref[at, cut(head)].astype(F32)
            inverse = lax.rsqrt(jnp.mean(mixture * mixture, axis=1, keepdims=True) + EPS)
            along = jnp.mean(wide * mixture, axis=1, keepdims=True) * inverse
            normed = mixture * inverse
            attended_ref[at, cut(j)] = normed.astype(BF16)
            mixgrad = (inverse * (wide - normed * along)).astype(BF16)
            mixgrad_ref[at, cut(j)] = mixgrad
            backs.append(mm(scaleds[p][i, b], mixgrad))
        back_ref[j] = backs[1]
        terms_ref[j] = k0 * backs[1] + backs[0]
        keep_ref[j : j + 1, :] = k0 * k1
    send_out(place, k, terms_ref, keep_ref, own_ref, send_ref)


def k4_body(head0, base, count, has_alias, place, query_ref, key_ref, value_ref, mixgrad_ref, attended_ref, grid_ref,
            turned_ref, weighted_ref, states_ref, enter_ref, *refs):
    key_part_ref, value_part_ref, attended_hbm, query_grad_hbm, query_grad_ref, sems = refs[2 * has_alias :]
    inner0 = head0 - base
    ours = slice(head0 * DH, (head0 + count) * DH)
    attend = pltpu.make_async_copy(
        attended_ref.at[:, inner0 * DH : (inner0 + count) * DH], attended_hbm.at[:, ours], sems.at[0]
    )
    attend.start()
    for j in range(count):
        head = head0 + j
        inner = head - base
        for b in range(2):
            at = block(b)
            mixgrad = mixgrad_ref[at, cut(inner)]
            value = value_ref[at, cut(inner)]
            masked = (mm(mixgrad, value, NT) * grid_ref[j, b]).astype(BF16)
            query_grad_ref[at, cut(j)] = (
                mm(masked, key_ref[at, cut(inner)]) + mm(mixgrad, states_ref[inner, b], NT) * enter_ref[at, cut(j)]
            ).astype(BF16)
            turned = (mm(value, mixgrad, NT) * turned_ref[j, b]).astype(BF16)
            key_part_ref[at, cut(j)] = mm(turned, query_ref[at, cut(head)])
            value_part_ref[at, cut(j)] = mm(weighted_ref[j, b], mixgrad)
    grads = pltpu.make_async_copy(query_grad_ref, query_grad_hbm.at[:, ours], sems.at[1])
    grads.start()
    attend.wait()
    grads.wait()


def k5_body(k, head0, pieces, per, has_alias, place, key_ref, value_ref, back_ref, rows_ref, mine_ref, other_ref,
            *refs):
    key_parts, value_parts, leaves = refs[:pieces], refs[pieces : 2 * pieces], refs[2 * pieces : 3 * pieces]
    key_grad_hbm, value_grad_hbm, key_grad_ref, value_grad_ref, state_ref, sems = refs[3 * pieces + 2 * has_alias :]
    take_in(place, k, mine_ref, other_ref, state_ref)
    copies = []
    for j in range(GROUPS * k):
        head = head0 + j
        p, i = j // per, j % per
        k0, k1 = keeps(rows_ref, head)
        outgoing = state_ref[j]
        afters = (k1 * outgoing + back_ref[j], outgoing)
        for b in range(2):
            at = block(b)
            low = afters[b].astype(BF16)
            leave = leaves[p][at, cut(i)]
            key_grad_ref[at, cut(j)] = (
                key_parts[p][at, cut(i)] + mm(value_ref[at, cut(j)], low, NT) * leave
            ).astype(BF16)
            value_grad_ref[at, cut(j)] = (
                value_parts[p][at, cut(i)] + mm(key_ref[at, cut(j)], low) * leave
            ).astype(BF16)
        for n, (source, target) in enumerate(((key_grad_ref, key_grad_hbm), (value_grad_ref, value_grad_hbm))):
            copy = pltpu.make_async_copy(source.at[:, cut(j)], target.at[:, cut(head)], sems.at[2 * j + n])
            copy.start()
            copies.append(copy)
    for copy in copies:
        copy.wait()


def joined(later, got_ref, held_ref, heads, j):
    one = slice(heads * DH + j, heads * DH + j + 1)
    a_got, a_held = got_ref[one, :], held_ref[one, :]
    state = jnp.where(later, a_held, 1.0) * got_ref[cut(j), :] + jnp.where(later, 1.0, a_got) * held_ref[cut(j), :]
    return state, a_got * a_held


def before(later, got_ref, prefix_ref, k, j):
    one = slice(k * DH + j, k * DH + j + 1)
    a_got = got_ref[one, :]
    if prefix_ref is None:
        return jnp.where(later, 1.0, 0.0) * got_ref[cut(j), :], jnp.where(later, a_got, 1.0)
    a = prefix_ref[one, :]
    state = jnp.where(later, a, 0.0) * got_ref[cut(j), :] + prefix_ref[cut(j), :]
    return state, jnp.where(later, a * a_got, a)


def put(out, heads, j, value):
    out[cut(j), :], out[heads * DH + j : heads * DH + j + 1, :] = value


def c1_body(turn, k, place, own_ref, got_ref, keep_ref, send_ref):
    later = (place[turn] & 1) == 1
    for out in (keep_ref, send_ref):
        out[k * DH :, :] = jnp.ones((8, DH), F32)
    for j in range(2 * k):
        put(keep_ref if j < k else send_ref, k, j % k, joined(later, got_ref, own_ref, 2 * k, j))


def c2_body(turn, k, place, own_ref, got_ref, total_ref):
    later = (place[turn] & 2) == 2
    total_ref[k * DH :, :] = jnp.ones((8, DH), F32)
    for j in range(k):
        put(total_ref, k, j, joined(later, got_ref, own_ref, k, j))


def cz_body(turn, k, bit, first, place, *refs):
    total_ref, got_ref = refs[:2]
    prefix_ref = None if first else refs[2]
    new_total_ref, new_prefix_ref = refs[-2:]
    later = (place[turn] & bit) == bit
    for out in (new_total_ref, new_prefix_ref):
        out[k * DH :, :] = jnp.ones((8, DH), F32)
    for j in range(k):
        put(new_total_ref, k, j, joined(later, got_ref, total_ref, k, j))
        put(new_prefix_ref, k, j, before(later, got_ref, prefix_ref, k, j))


def c3_body(turn, k, bit, first, place, *refs):
    got_ref = refs[0]
    prefix_ref = None if first else refs[1]
    own_ref, chip_ref, mine_ref, send_ref = refs[-4:]
    later = (place[turn] & bit) == bit
    upper = (place[turn] & 2) == 2
    for j in range(k):
        at, one = cut(j), slice(k * DH + j, k * DH + j + 1)
        prefix, _ = before(later, got_ref, prefix_ref, k, j)
        mine_ref[at, :] = jnp.where(upper, chip_ref[one, :], 1.0) * prefix + jnp.where(upper, 1.0, 0.0) * chip_ref[at, :]
        send_ref[at, :] = jnp.where(upper, 1.0, own_ref[one, :]) * prefix + jnp.where(upper, 0.0, 1.0) * own_ref[at, :]


def c4_body(turn, k, place, half_ref, got_half_ref, own_ref, got_ref, mine_ref, send_ref):
    later = (place[turn] & 1) == 1
    for j in range(2 * k):
        at, one = cut(j), slice(2 * k * DH + j, 2 * k * DH + j + 1)
        chip = half_ref[cut(j), :] if j < k else got_half_ref[cut(j - k), :]
        mine_ref[at, :] = jnp.where(later, got_ref[one, :], 1.0) * chip + jnp.where(later, 1.0, 0.0) * got_ref[at, :]
        send_ref[at, :] = jnp.where(later, 1.0, own_ref[one, :]) * chip + jnp.where(later, 0.0, 1.0) * own_ref[at, :]


def exchange(x, bit, count):
    return lax.ppermute(x, "seq", [(i, i ^ bit) for i in range(count)])


class Order:
    def __init__(self, place):
        self.place, self.last = place, ()

    def __call__(self, body, inside, outs, **options):
        taken = [id(a) for a in options.get("outside", ())]
        after = tuple(a for a in self.last if id(a) not in taken)
        out = run(body, self.place, inside, outs, after=after, **options)
        self.last = (out[0],)
        return out


def scan_devices(call, own, send, turn, k, count):
    half = ((k * DH + 8, DH), F32)
    got = exchange(send, 1, count)
    yield
    chip, chip_send = call(functools.partial(c1_body, turn, k), (own, got), (half, half))
    chip_got = exchange(chip_send, 2, count)
    yield
    (total,) = call(functools.partial(c2_body, turn, k), (chip, chip_got), (half,))
    prefix = ()
    bit = 4
    while bit < count:
        got_total = exchange(total, bit, count)
        yield
        if bit * 2 < count:
            body = functools.partial(cz_body, turn, k, bit, not prefix)
            total, *prefix = call(body, (total, got_total, *prefix), (half, half))
        else:
            body = functools.partial(c3_body, turn, k, bit, not prefix)
            mine, mine_send = call(body, (got_total, *prefix, chip, chip_got), (((k * DH, DH), F32),) * 2)
        bit *= 2
    mine_got = exchange(mine_send, 2, count)
    yield
    body = functools.partial(c4_body, turn, k)
    state, state_send = call(body, (mine, mine_got, own, got), (((2 * k * DH, DH), F32),) * 2)
    yield state, exchange(state_send, 1, count)


def drive(scans, fillers):
    fillers = list(fillers)
    step = 0
    while True:
        results = [next(scan) for scan in scans]
        if results[0] is not None:
            break
        if step and fillers:
            fillers.pop(0)()
        step += 1
    for filler in fillers:
        filler()
    return results


def local(query_rows, key_rows, value_rows, log_decay, run_start, out_grad):
    all_heads = log_decay.shape[0]
    tokens, width = query_rows.shape
    count = lax.axis_size("seq")
    seat = lax.axis_index("seq")
    place = jnp.stack([((seat & 1) << 1) | ((seat >> 1) & 1), seat, count - 1 - seat])
    call = Order(place)
    heads = all_heads // CHUNKS
    k = heads // GROUPS
    per = heads // PIECES
    chunks = range(CHUNKS)
    dma = pltpu.SemaphoreType.DMA
    message = ((2 * k * DH + 8, DH), F32)
    states = ((heads, DH, DH), F32)
    flat = jax.ShapeDtypeStruct((tokens, width), BF16)
    chunk_bf16 = ((tokens, heads * DH), BF16)
    piece_f32 = ((tokens, per * DH), F32)
    square = (per, 2, BLOCK, BLOCK)
    mask = ((2, BLOCK, BLOCK), F32)
    scratch_terms = (pltpu.VMEM((heads, DH, DH), F32), pltpu.VMEM((8, DH), F32))

    own, send, loc, keys, values, scans = [], [], [], [], [], []
    for c in chunks:
        outs = (message, message, states, chunk_bf16, chunk_bf16)
        scratch = scratch_terms + (dma((2 * heads + 2,)),)
        if c == 0:
            outs += (((32, tokens), F32), ((tokens, DH), F32))
            scratch += (pltpu.VMEM(log_decay.shape, F32), pltpu.VMEM((1, tokens), jnp.int32))
            inside, outside = (), (log_decay, run_start.reshape(1, tokens), key_rows, value_rows)
        else:
            inside, outside = (rows,), (key_rows, value_rows)
        out = call(functools.partial(k1_body, k, c * heads), inside, outs, outside=outside, scratch=scratch)
        if c == 0:
            rows, cols = out[5:]
        own.append(out[0])
        send.append(out[1])
        loc.append(out[2])
        keys.append(out[3])
        values.append(out[4])
        scans.append(scan_devices(call, out[0], out[1], 1, k, count))

    forward = []

    def k2(n):
        c = n // PIECES
        outs = (piece_f32, (square, F32), (square, F32), (square, BF16), ((per, 2, DH, BLOCK), BF16))
        outs += (piece_f32, piece_f32)
        inputs = (query_rows, keys[c], values[c], rows, cols)
        if n == 0:
            outs += (mask, mask)
        else:
            inputs += tuple(forward[0][7:])
        forward.append(call(functools.partial(k2_body, n == 0, n * per, c * heads, per), inputs, outs))

    fillers = range(CHUNKS * PIECES)
    results = drive(scans, [functools.partial(k2, n) for n in fillers])
    middle, scans = [], []
    for c, (mine, other) in enumerate(results):
        mid = forward[c * PIECES : (c + 1) * PIECES]
        out = call(
            functools.partial(k3_body, k, c * heads, PIECES, per),
            (query_rows, out_grad, loc[c], rows, mine, other)
            + tuple(f[0] for f in mid) + tuple(f[4] for f in mid) + tuple(f[5] for f in mid),
            (message, message, chunk_bf16, ((heads, 2, DH, DH), BF16), states, chunk_bf16),
            scratch=scratch_terms + (pltpu.VMEM((heads, DH, DH), F32),),
        )
        middle.append(out)
        scans.append(scan_devices(call, out[0], out[1], 2, k, count))

    backward = []

    def k4(n):
        c = n // PIECES
        _, _, mixgrad, states_low, _, attended = middle[c]
        f = forward[n]
        backward.append(
            call(
                functools.partial(k4_body, n * per, c * heads, per, int(n > 0)),
                (query_rows, keys[c], values[c], mixgrad, attended, f[1], f[2], f[3], states_low, f[5]),
                (piece_f32, piece_f32, flat, flat),
                outside=tuple(backward[-1][2:]) if backward else (),
                aliases={0: 2, 1: 3} if backward else None,
                scratch=(pltpu.VMEM((tokens, per * DH), BF16), dma((2,))),
            )
        )

    results = drive(scans, [functools.partial(k4, n) for n in fillers])
    grads = ()
    for c, (mine, other) in enumerate(results):
        back = backward[c * PIECES : (c + 1) * PIECES]
        mid = forward[c * PIECES : (c + 1) * PIECES]
        grads = call(
            functools.partial(k5_body, k, c * heads, PIECES, per, int(c > 0)),
            (keys[c], values[c], middle[c][4], rows, mine, other)
            + tuple(b[0] for b in back) + tuple(b[1] for b in back) + tuple(f[6] for f in mid),
            (flat, flat),
            outside=tuple(grads),
            aliases={0: 0, 1: 1} if grads else None,
            scratch=(pltpu.VMEM((tokens, heads * DH), BF16),) * 2
            + (pltpu.VMEM((heads, DH, DH), F32), dma((2 * heads,))),
        )
    return (*backward[-1][2:], *grads)


def solution(mesh):
    rows = P(("groups", "seq"), None)
    return jax.shard_map(
        local,
        mesh=mesh,
        in_specs=(rows, rows, rows, P(None, ("groups", "seq")), P(("groups", "seq")), rows),
        out_specs=(rows, rows, rows, rows),
        check_vma=False,
    )
```

```python
import functools

import jax
import jax.numpy as jnp
from jax import lax
from jax.experimental import pallas as pl
from jax.experimental.pallas import tpu as pltpu
from jax.sharding import PartitionSpec as P

BLOCK = 256
HALF = 128
DH = 128
EPS = 1e-05
FAR = -1e30
GROUPS = 4
CHUNKS = 2
PIECES = 2
F32 = jnp.float32
BF16 = jnp.bfloat16

NN = (((1,), (0,)), ((), ()))
NT = (((1,), (1,)), ((), ()))
TN = (((0,), (0,)), ((), ()))


def mm(a, b, dims=NN):
    return lax.dot_general(a, b, dims, preferred_element_type=F32)


def cut(j):
    return slice(j * DH, (j + 1) * DH)


def block(b):
    return slice(b * BLOCK, (b + 1) * BLOCK)


def group_of(place):
    return ((place[0] & 1) << 1) | ((place[0] >> 1) & 1)


def position(place, backward):
    return ~place[0] if backward else place[0]


SMEM = pl.BlockSpec(memory_space=pltpu.SMEM)
VMEM = pl.BlockSpec(memory_space=pltpu.VMEM)
ANY = pl.BlockSpec(memory_space=pl.ANY)
HBM = pl.BlockSpec(memory_space=pltpu.HBM)


def run(body, scalar, inside, outs, outside=(), after=(), aliases=None, scratch=(), megabytes=8):
    taken = len(inside) + len(outside)

    def kernel(scalar_ref, *refs):
        body(scalar_ref, *refs[:taken], *refs[taken + len(after) :])

    shapes = [pltpu.HBM(o.shape, o.dtype) if isinstance(o, jax.ShapeDtypeStruct) else pltpu.VMEM(*o) for o in outs]
    return pl.pallas_call(
        kernel,
        in_specs=[SMEM] + [VMEM] * len(inside) + [HBM] * len(outside) + [ANY] * len(after),
        out_specs=[HBM if isinstance(o, jax.ShapeDtypeStruct) else VMEM for o in outs],
        out_shape=shapes,
        input_output_aliases={1 + len(inside) + i: o for i, o in (aliases or {}).items()},
        scratch_shapes=list(scratch),
        compiler_params=pltpu.CompilerParams(vmem_limit_bytes=megabytes << 20),
    )(scalar, *[pltpu.with_memory_space_constraint(a, pltpu.VMEM) for a in inside],
      *[pltpu.with_memory_space_constraint(a, pltpu.HBM) for a in outside], *after)


def prepare(decay_ref, start_ref, rows_ref, cols_ref):
    tri = (
        lax.broadcasted_iota(jnp.int32, (BLOCK, BLOCK), 0) <= lax.broadcasted_iota(jnp.int32, (BLOCK, BLOCK), 1)
    ).astype(F32)
    for b in range(decay_ref.shape[1] // BLOCK):
        at = block(b)
        starts = jnp.broadcast_to(start_ref[:, at].astype(F32), (8, BLOCK))
        both = jnp.concatenate([decay_ref[:, at], starts], axis=0)
        sums = lax.dot_general(both, tri, NN, precision=lax.Precision.HIGHEST, preferred_element_type=F32)
        cumul, marks = sums[:8], sums[8:]
        last, last_mark = cumul[:, BLOCK - 1 :], marks[:, BLOCK - 1 :]
        entering = jnp.where(marks == 0.0, jnp.exp(cumul), 0.0)
        leaving = jnp.where(marks == last_mark, jnp.exp(last - cumul), 0.0)
        stack = jnp.concatenate([cumul, entering, leaving, marks], axis=0)
        rows_ref[:, at] = stack
        cols_ref[at, :] = jnp.concatenate([stack, jnp.zeros((96, BLOCK), F32)], axis=0).T


def keeps(rows_ref, head):
    enter = rows_ref[8 + head : 9 + head, :]
    k0 = jnp.broadcast_to(enter[:, BLOCK - 1 : BLOCK], (1, DH))
    k1 = jnp.broadcast_to(enter[:, 2 * BLOCK - 1 : 2 * BLOCK], (1, DH))
    return k0, k1


def send_out(place, k, terms_ref, keep_ref, own_ref, send_ref):
    for out, first in ((own_ref, 0), (send_ref, 2 * k)):
        for r in range(2 * k):
            group, j = (first + r) // k, (first + r) % k
            head = (group ^ group_of(place)) * k + j
            out[cut(r), :] = terms_ref[head]
            out[pl.ds(2 * k * DH + r, 1), :] = keep_ref[pl.ds(head, 1), :]
        rest = 8 - 2 * k
        out[2 * k * DH + 2 * k :, :] = jnp.ones((rest, DH), F32)


def take_in(place, k, mine_ref, other_ref, state_ref):
    for r in range(GROUPS * k):
        source = mine_ref if r < 2 * k else other_ref
        state_ref[((r // k) ^ group_of(place)) * k + r % k] = source[cut(r % (2 * k)), :]


def k1_body(k, head0, chunks, place, *refs):
    heads = GROUPS * k
    if head0 == 0:
        decay_hbm, start_hbm, key_hbm, value_hbm, own_ref, send_ref, loc_ref, rows_ref, cols_ref = refs[:9]
        copied = refs[9 : 9 + 2 * chunks]
        terms_ref, keep_ref, decay_ref, start_ref, sems = refs[9 + 2 * chunks :]
        loads = [
            pltpu.make_async_copy(decay_hbm, decay_ref, sems.at[0]),
            pltpu.make_async_copy(start_hbm, start_ref, sems.at[1]),
        ]
        for n, target in enumerate(copied):
            source, first = (key_hbm, value_hbm)[n % 2], n // 2 * heads * DH
            loads.append(pltpu.make_async_copy(source.at[:, first : first + heads * DH], target, sems.at[2 + n]))
        for load in loads:
            load.start()
        loads[0].wait()
        loads[1].wait()
        prepare(decay_ref, start_ref, rows_ref, cols_ref)
        loads[2].wait()
        loads[3].wait()
        key_ref, value_ref = copied[:2]
    else:
        rows_ref, key_ref, value_ref, own_ref, send_ref, loc_ref, terms_ref, keep_ref = refs
        loads = []
    for j in range(heads):
        head = head0 + j
        leave = rows_ref[16 + head : 17 + head, :]
        terms = []
        for b in range(2):
            keys = key_ref[block(b), cut(j)].T.astype(F32)
            scaled = (keys * leave[:, block(b)]).astype(BF16)
            terms.append(mm(scaled, value_ref[block(b), cut(j)]))
        k0, k1 = keeps(rows_ref, head)
        loc_ref[j] = terms[0]
        terms_ref[j] = k1 * terms[0] + terms[1]
        keep_ref[j : j + 1, :] = k0 * k1
    send_out(place, k, terms_ref, keep_ref, own_ref, send_ref)
    for load in loads[4:]:
        load.wait()


def make_bias(rows_ref, cols_ref, bias_ref, turned_ref):
    down = lax.broadcasted_iota(jnp.int32, (BLOCK, BLOCK), 0)
    along = lax.broadcasted_iota(jnp.int32, (BLOCK, BLOCK), 1)
    for b in range(2):
        same = cols_ref[block(b), 24:25] == rows_ref[24:25, block(b)]
        bias_ref[b] = jnp.where((down >= along) & same, 0.0, FAR)
        turned_ref[b] = jnp.where((down <= along) & same, 0.0, FAR)


def k2_body(first, head0, base, count, place, query_ref, key_ref, value_ref, rows_ref, cols_ref, *refs):
    if first:
        (within_ref, grid_ref, turned_ref, weighted_ref, scaled_ref, enter_ref, leave_ref,
         bias_ref, bias_turned_ref) = refs
        make_bias(rows_ref, cols_ref, bias_ref, bias_turned_ref)
    else:
        (bias_ref, bias_turned_ref, within_ref, grid_ref, turned_ref, weighted_ref, scaled_ref, enter_ref,
         leave_ref) = refs
    zeros = jnp.zeros((HALF, HALF), F32)
    for j in range(count):
        head = head0 + j
        inner = head - base
        for b in range(2):
            at = block(b)
            query, key = query_ref[at, cut(head)], key_ref[at, cut(inner)]
            cum_row = rows_ref[head : head + 1, at]
            top, low = slice(0, HALF), slice(HALF, BLOCK)
            cum_top = jnp.broadcast_to(cols_ref[b * BLOCK : b * BLOCK + HALF, head : head + 1], (HALF, HALF))
            cum_low = jnp.broadcast_to(cols_ref[b * BLOCK + HALF : (b + 1) * BLOCK, head : head + 1], (HALF, HALF))
            row_top, row_low = cum_row[:, :HALF], cum_row[:, HALF:]

            def decay(difference, limit):
                return jnp.exp(jnp.minimum(difference, limit))

            grid_ref[j, b, top, top] = decay(cum_top - row_top, bias_ref[b, top, top])
            grid_ref[j, b, low, top] = decay(cum_low - row_top, bias_ref[b, low, top])
            grid_ref[j, b, low, low] = decay(cum_low - row_low, bias_ref[b, low, low])
            grid_ref[j, b, top, low] = zeros
            turned_ref[j, b, top, top] = decay(row_top - cum_top, bias_turned_ref[b, top, top])
            turned_ref[j, b, top, low] = decay(row_low - cum_top, bias_turned_ref[b, top, low])
            turned_ref[j, b, low, low] = decay(row_low - cum_low, bias_turned_ref[b, low, low])
            turned_ref[j, b, low, top] = zeros
            weighted = (mm(query, key, NT) * grid_ref[j, b]).astype(BF16)
            weighted_ref[j, b] = (mm(key, query, NT) * turned_ref[j, b]).astype(BF16)
            within_ref[at, cut(j)] = mm(weighted, value_ref[at, cut(inner)])
            enter = rows_ref[8 + head : 9 + head, at]
            scaled_ref[j, b] = (query.T.astype(F32) * enter).astype(BF16)
            enter_ref[at, cut(j)] = jnp.broadcast_to(cols_ref[at, 8 + head : 9 + head], (BLOCK, DH))
            leave_ref[at, cut(j)] = jnp.broadcast_to(cols_ref[at, 16 + head : 17 + head], (BLOCK, DH))


def k3_body(k, head0, pieces, per, place, query_ref, grad_ref, loc_ref, rows_ref, mine_ref, other_ref, *refs):
    withins, scaleds, enters = refs[:pieces], refs[pieces : 2 * pieces], refs[2 * pieces : 3 * pieces]
    own_ref, send_ref, mixgrad_ref, states_ref, back_ref, attended_ref = refs[3 * pieces : 3 * pieces + 6]
    terms_ref, keep_ref, state_ref = refs[3 * pieces + 6 :]
    take_in(place, k, mine_ref, other_ref, state_ref)
    for j in range(GROUPS * k):
        head = head0 + j
        p, i = j // per, j % per
        k0, k1 = keeps(rows_ref, head)
        incoming = state_ref[j]
        states = (incoming, k0 * incoming + loc_ref[j])
        backs = []
        for b in range(2):
            at = block(b)
            low = states[b].astype(BF16)
            states_ref[j, b] = low
            mixture = withins[p][at, cut(i)] + mm(query_ref[at, cut(head)], low) * enters[p][at, cut(i)]
            wide = grad_ref[at, cut(head)].astype(F32)
            inverse = lax.rsqrt(jnp.mean(mixture * mixture, axis=1, keepdims=True) + EPS)
            along = jnp.mean(wide * mixture, axis=1, keepdims=True) * inverse
            normed = mixture * inverse
            attended_ref[at, cut(j)] = normed.astype(BF16)
            mixgrad = (inverse * (wide - normed * along)).astype(BF16)
            mixgrad_ref[at, cut(j)] = mixgrad
            backs.append(mm(scaleds[p][i, b], mixgrad))
        back_ref[j] = backs[1]
        terms_ref[j] = k0 * backs[1] + backs[0]
        keep_ref[j : j + 1, :] = k0 * k1
    send_out(place, k, terms_ref, keep_ref, own_ref, send_ref)


def columns(ref, first, count):
    return ref.at[:, first * DH : (first + count) * DH]


def k4_body(head0, base, count, place, query_ref, key_ref, value_ref, mixgrad_ref, attended_ref, grid_ref,
            turned_ref, weighted_ref, states_ref, enter_ref, *refs):
    later = head0 > 0
    key_part_ref, value_part_ref, query_grad_ref, attended_hbm, query_grad_hbm, sems = refs[3 * later :]
    inner0 = head0 - base
    copies = [
        pltpu.make_async_copy(
            columns(attended_ref, inner0, count), columns(attended_hbm, head0, count), sems.at[0]
        )
    ]
    if later:
        copies.append(
            pltpu.make_async_copy(refs[0], columns(query_grad_hbm, head0 - count, count), sems.at[1])
        )
    for copy in copies:
        copy.start()
    for j in range(count):
        head = head0 + j
        inner = head - base
        for b in range(2):
            at = block(b)
            mixgrad = mixgrad_ref[at, cut(inner)]
            value = value_ref[at, cut(inner)]
            masked = (mm(mixgrad, value, NT) * grid_ref[j, b]).astype(BF16)
            query_grad_ref[at, cut(j)] = (
                mm(masked, key_ref[at, cut(inner)]) + mm(mixgrad, states_ref[inner, b], NT) * enter_ref[at, cut(j)]
            ).astype(BF16)
            turned = (mm(value, mixgrad, NT) * turned_ref[j, b]).astype(BF16)
            key_part_ref[at, cut(j)] = mm(turned, query_ref[at, cut(head)])
            value_part_ref[at, cut(j)] = mm(weighted_ref[j, b], mixgrad)
    for copy in copies:
        copy.wait()


def k5_body(k, head0, pieces, per, chunks, place, key_ref, value_ref, back_ref, rows_ref, mine_ref, other_ref, *refs):
    heads = GROUPS * k
    key_parts, value_parts, leaves = refs[:pieces], refs[pieces : 2 * pieces], refs[2 * pieces : 3 * pieces]
    refs = refs[3 * pieces :]
    first, last = head0 == 0, head0 == (chunks - 1) * heads
    copies = []
    if first:
        done_ref, refs = refs[0], refs[2:]
    earlier, refs = refs[: 2 * (chunks - 1) * last], refs[2 * (chunks - 1) * last :]
    if last:
        key_grad_hbm, value_grad_hbm, refs = refs[0], refs[1], refs[2:]
    else:
        key_grad_ref, value_grad_ref, refs = refs[0], refs[1], refs[2:]
    if first:
        query_grad_hbm, refs = refs[0], refs[1:]
    state_ref, sems, refs = refs[0], refs[1], refs[2:]
    if last:
        key_grad_ref, value_grad_ref = refs

    def ship(source, target):
        copy = pltpu.make_async_copy(source, target, sems.at[len(copies)])
        copy.start()
        copies.append(copy)

    if first:
        ship(done_ref, columns(query_grad_hbm, chunks * heads - per, per))
    for n in range(0, len(earlier), 2):
        ship(earlier[n], columns(key_grad_hbm, n // 2 * heads, heads))
        ship(earlier[n + 1], columns(value_grad_hbm, n // 2 * heads, heads))
    take_in(place, k, mine_ref, other_ref, state_ref)
    for j in range(heads):
        head = head0 + j
        p, i = j // per, j % per
        k0, k1 = keeps(rows_ref, head)
        outgoing = state_ref[j]
        afters = (k1 * outgoing + back_ref[j], outgoing)
        for b in range(2):
            at = block(b)
            low = afters[b].astype(BF16)
            leave = leaves[p][at, cut(i)]
            key_grad_ref[at, cut(j)] = (
                key_parts[p][at, cut(i)] + mm(value_ref[at, cut(j)], low, NT) * leave
            ).astype(BF16)
            value_grad_ref[at, cut(j)] = (
                value_parts[p][at, cut(i)] + mm(key_ref[at, cut(j)], low) * leave
            ).astype(BF16)
        if last:
            ship(columns(key_grad_ref, j, 1), columns(key_grad_hbm, head, 1))
            ship(columns(value_grad_ref, j, 1), columns(value_grad_hbm, head, 1))
    for copy in copies:
        copy.wait()


def joined(later, got_ref, held_ref, heads, j):
    one = slice(heads * DH + j, heads * DH + j + 1)
    a_got, a_held = got_ref[one, :], held_ref[one, :]
    state = jnp.where(later, a_held, 1.0) * got_ref[cut(j), :] + jnp.where(later, 1.0, a_got) * held_ref[cut(j), :]
    return state, a_got * a_held


def before(later, got_ref, prefix_ref, k, j):
    one = slice(k * DH + j, k * DH + j + 1)
    a_got = got_ref[one, :]
    if prefix_ref is None:
        return jnp.where(later, 1.0, 0.0) * got_ref[cut(j), :], jnp.where(later, a_got, 1.0)
    a = prefix_ref[one, :]
    state = jnp.where(later, a, 0.0) * got_ref[cut(j), :] + prefix_ref[cut(j), :]
    return state, jnp.where(later, a * a_got, a)


def put(out, heads, j, value):
    out[cut(j), :], out[heads * DH + j : heads * DH + j + 1, :] = value


def c1_body(turn, k, place, own_ref, got_ref, keep_ref, send_ref):
    later = (position(place, turn) & 1) == 1
    for out in (keep_ref, send_ref):
        out[k * DH :, :] = jnp.ones((8, DH), F32)
    for j in range(2 * k):
        put(keep_ref if j < k else send_ref, k, j % k, joined(later, got_ref, own_ref, 2 * k, j))


def c2_body(turn, k, place, own_ref, got_ref, total_ref):
    later = (position(place, turn) & 2) == 2
    total_ref[k * DH :, :] = jnp.ones((8, DH), F32)
    for j in range(k):
        put(total_ref, k, j, joined(later, got_ref, own_ref, k, j))


def cz_body(turn, k, bit, first, place, *refs):
    total_ref, got_ref = refs[:2]
    prefix_ref = None if first else refs[2]
    new_total_ref, new_prefix_ref = refs[-2:]
    later = (position(place, turn) & bit) == bit
    for out in (new_total_ref, new_prefix_ref):
        out[k * DH :, :] = jnp.ones((8, DH), F32)
    for j in range(k):
        put(new_total_ref, k, j, joined(later, got_ref, total_ref, k, j))
        put(new_prefix_ref, k, j, before(later, got_ref, prefix_ref, k, j))


def c3_body(turn, k, bit, first, place, *refs):
    got_ref = refs[0]
    prefix_ref = None if first else refs[1]
    own_ref, chip_ref, mine_ref, send_ref = refs[-4:]
    later = (position(place, turn) & bit) == bit
    upper = (position(place, turn) & 2) == 2
    for j in range(k):
        at, one = cut(j), slice(k * DH + j, k * DH + j + 1)
        prefix, _ = before(later, got_ref, prefix_ref, k, j)
        mine_ref[at, :] = jnp.where(upper, chip_ref[one, :], 1.0) * prefix + jnp.where(upper, 1.0, 0.0) * chip_ref[at, :]
        send_ref[at, :] = jnp.where(upper, 1.0, own_ref[one, :]) * prefix + jnp.where(upper, 0.0, 1.0) * own_ref[at, :]


def c4_body(turn, k, place, half_ref, got_half_ref, own_ref, got_ref, mine_ref, send_ref):
    later = (position(place, turn) & 1) == 1
    for j in range(2 * k):
        at, one = cut(j), slice(2 * k * DH + j, 2 * k * DH + j + 1)
        chip = half_ref[cut(j), :] if j < k else got_half_ref[cut(j - k), :]
        mine_ref[at, :] = jnp.where(later, got_ref[one, :], 1.0) * chip + jnp.where(later, 1.0, 0.0) * got_ref[at, :]
        send_ref[at, :] = jnp.where(later, 1.0, own_ref[one, :]) * chip + jnp.where(later, 0.0, 1.0) * own_ref[at, :]


def exchange(x, bit, count):
    return lax.ppermute(x, "seq", [(i, i ^ bit) for i in range(count)])


class Order:
    def __init__(self, place):
        self.place, self.last = place, ()

    def __call__(self, body, inside, outs, **options):
        taken = [id(a) for a in options.get("outside", ())]
        after = tuple(a for a in self.last if id(a) not in taken)
        out = run(body, self.place, inside, outs, after=after, **options)
        self.last = (out[0],)
        return out


def scan_devices(call, own, send, turn, k, count):
    half = ((k * DH + 8, DH), F32)
    got = exchange(send, 1, count)
    yield
    chip, chip_send = call(functools.partial(c1_body, turn, k), (own, got), (half, half))
    chip_got = exchange(chip_send, 2, count)
    yield
    (total,) = call(functools.partial(c2_body, turn, k), (chip, chip_got), (half,))
    prefix = ()
    bit = 4
    while bit < count:
        got_total = exchange(total, bit, count)
        yield
        if bit * 2 < count:
            body = functools.partial(cz_body, turn, k, bit, not prefix)
            total, *prefix = call(body, (total, got_total, *prefix), (half, half))
        else:
            body = functools.partial(c3_body, turn, k, bit, not prefix)
            mine, mine_send = call(body, (got_total, *prefix, chip, chip_got), (((k * DH, DH), F32),) * 2)
        bit *= 2
    mine_got = exchange(mine_send, 2, count)
    yield
    body = functools.partial(c4_body, turn, k)
    state, state_send = call(body, (mine, mine_got, own, got), (((2 * k * DH, DH), F32),) * 2)
    yield state, exchange(state_send, 1, count)


def drive(scans, fillers):
    fillers = list(fillers)
    step = 0
    while True:
        results = [next(scan) for scan in scans]
        if results[0] is not None:
            break
        if step and fillers:
            fillers.pop(0)()
        step += 1
    for filler in fillers:
        filler()
    return results


def local(query_rows, key_rows, value_rows, log_decay, run_start, out_grad):
    all_heads = log_decay.shape[0]
    tokens, width = query_rows.shape
    count = lax.axis_size("seq")
    seat = lax.axis_index("seq")
    call = Order(seat.reshape(1))
    heads = all_heads // CHUNKS
    k = heads // GROUPS
    per = heads // PIECES
    chunks = range(CHUNKS)
    dma = pltpu.SemaphoreType.DMA
    message = ((2 * k * DH + 8, DH), F32)
    states = ((heads, DH, DH), F32)
    flat = jax.ShapeDtypeStruct((tokens, width), BF16)
    chunk_bf16 = ((tokens, heads * DH), BF16)
    piece_f32 = ((tokens, per * DH), F32)
    square = (per, 2, BLOCK, BLOCK)
    mask = ((2, BLOCK, BLOCK), F32)
    scratch_terms = (pltpu.VMEM((heads, DH, DH), F32), pltpu.VMEM((8, DH), F32))

    loc, scans = [], []
    for c in chunks:
        outs = (message, message, states)
        scratch = scratch_terms
        body = functools.partial(k1_body, k, c * heads, CHUNKS)
        if c == 0:
            outs += (((32, tokens), F32), ((tokens, DH), F32)) + (chunk_bf16,) * (2 * CHUNKS)
            scratch += (pltpu.VMEM(log_decay.shape, F32), pltpu.VMEM((1, tokens), jnp.int32), dma((2 * CHUNKS + 2,)))
            outside = (log_decay, run_start.reshape(1, tokens), key_rows, value_rows)
            out = call(body, (), outs, outside=outside, scratch=scratch)
            rows, cols = out[3:5]
            keys, values = out[5::2], out[6::2]
        else:
            out = call(body, (rows, keys[c], values[c]), outs, scratch=scratch)
        loc.append(out[2])
        scans.append(scan_devices(call, out[0], out[1], False, k, count))

    forward = []

    def k2(n):
        c = n // PIECES
        outs = (piece_f32, (square, F32), (square, F32), (square, BF16), ((per, 2, DH, BLOCK), BF16))
        outs += (piece_f32, piece_f32)
        inputs = (query_rows, keys[c], values[c], rows, cols)
        if n == 0:
            outs += (mask, mask)
        else:
            inputs += tuple(forward[0][7:])
        forward.append(call(functools.partial(k2_body, n == 0, n * per, c * heads, per), inputs, outs))

    fillers = range(CHUNKS * PIECES)
    results = drive(scans, [functools.partial(k2, n) for n in fillers])
    middle, scans = [], []
    for c, (mine, other) in enumerate(results):
        mid = forward[c * PIECES : (c + 1) * PIECES]
        out = call(
            functools.partial(k3_body, k, c * heads, PIECES, per),
            (query_rows, out_grad, loc[c], rows, mine, other)
            + tuple(f[0] for f in mid) + tuple(f[4] for f in mid) + tuple(f[5] for f in mid),
            (message, message, chunk_bf16, ((heads, 2, DH, DH), BF16), states, chunk_bf16),
            scratch=scratch_terms + (pltpu.VMEM((heads, DH, DH), F32),),
        )
        middle.append(out)
        scans.append(scan_devices(call, out[0], out[1], True, k, count))

    backward = []

    def k4(n):
        c = n // PIECES
        _, _, mixgrad, states_low, _, attended = middle[c]
        f = forward[n]
        backward.append(
            call(
                functools.partial(k4_body, n * per, c * heads, per),
                (query_rows, keys[c], values[c], mixgrad, attended, f[1], f[2], f[3], states_low, f[5])
                + ((backward[-1][2],) if n else ()),
                (piece_f32, piece_f32, ((tokens, per * DH), BF16), flat, flat),
                outside=tuple(backward[-1][3:]) if n else (),
                aliases={0: 3, 1: 4} if n else None,
                scratch=(dma((2,)),),
            )
        )

    results = drive(scans, [functools.partial(k4, n) for n in fillers])
    attended, query_grad = backward[-1][3:]
    grads = ()
    for c, (mine, other) in enumerate(results):
        first, last = c == 0, c == CHUNKS - 1
        back = backward[c * PIECES : (c + 1) * PIECES]
        mid = forward[c * PIECES : (c + 1) * PIECES]
        out = call(
            functools.partial(k5_body, k, c * heads, PIECES, per, CHUNKS),
            (keys[c], values[c], middle[c][4], rows, mine, other)
            + tuple(b[0] for b in back) + tuple(b[1] for b in back) + tuple(f[6] for f in mid)
            + ((backward[-1][2],) if first else ()) + (grads if last else ()),
            ((flat,) * 2 if last else (chunk_bf16,) * 2) + ((flat,) if first else ()),
            outside=(query_grad,) if first else (),
            aliases={0: 2} if first else None,
            scratch=(pltpu.VMEM((heads, DH, DH), F32), dma((2 * heads + 2 * CHUNKS,)))
            + ((pltpu.VMEM((tokens, heads * DH), BF16),) * 2 if last else ()),
        )
        if first:
            query_grad = out[2]
        grads = grads + tuple(out[:2])
    return attended, query_grad, out[0], out[1]


def solution(mesh):
    rows = P(("groups", "seq"), None)
    return jax.shard_map(
        local,
        mesh=mesh,
        in_specs=(rows, rows, rows, P(None, ("groups", "seq")), P(("groups", "seq")), rows),
        out_specs=(rows, rows, rows, rows),
        check_vma=False,
    )
```

```python
import functools

import jax
import jax.numpy as jnp
from jax import lax
from jax.experimental import pallas as pl
from jax.experimental.pallas import tpu as pltpu
from jax.sharding import PartitionSpec as P

BLOCK = 256
HALF = 128
DH = 128
EPS = 1e-05
FAR = -1e30
GROUPS = 4
CHUNKS = 2
K3_TURNS = ((0, 0), (0, 1), (1, 1))
K5_TURNS = ((0, 0), (0, 1), (1, 0), (1, 1))
PIECES = 2
F32 = jnp.float32
BF16 = jnp.bfloat16

NN = (((1,), (0,)), ((), ()))
NT = (((1,), (1,)), ((), ()))
TN = (((0,), (0,)), ((), ()))


def mm(a, b, dims=NN):
    return lax.dot_general(a, b, dims, preferred_element_type=F32)


def cut(j):
    return slice(j * DH, (j + 1) * DH)


def block(b):
    return slice(b * BLOCK, (b + 1) * BLOCK)


def group_of(place):
    return ((place[0] & 1) << 1) | ((place[0] >> 1) & 1)


def position(place, backward):
    return ~place[0] if backward else place[0]


SMEM = pl.BlockSpec(memory_space=pltpu.SMEM)
VMEM = pl.BlockSpec(memory_space=pltpu.VMEM)
ANY = pl.BlockSpec(memory_space=pl.ANY)
HBM = pl.BlockSpec(memory_space=pltpu.HBM)


def run(body, scalar, inside, outs, outside=(), after=(), aliases=None, renewed=None, scratch=(), megabytes=8):
    taken = len(inside) + len(outside)

    def kernel(scalar_ref, *refs):
        body(scalar_ref, *refs[:taken], *refs[taken + len(after) :])

    shapes = [pltpu.HBM(o.shape, o.dtype) if isinstance(o, jax.ShapeDtypeStruct) else pltpu.VMEM(*o) for o in outs]
    return pl.pallas_call(
        kernel,
        in_specs=[SMEM] + [VMEM] * len(inside) + [HBM] * len(outside) + [ANY] * len(after),
        out_specs=[HBM if isinstance(o, jax.ShapeDtypeStruct) else VMEM for o in outs],
        out_shape=shapes,
        input_output_aliases={1 + len(inside) + i: o for i, o in (aliases or {}).items()}
        | {1 + i: o for i, o in (renewed or {}).items()},
        scratch_shapes=list(scratch),
        compiler_params=pltpu.CompilerParams(vmem_limit_bytes=megabytes << 20),
    )(scalar, *[pltpu.with_memory_space_constraint(a, pltpu.VMEM) for a in inside],
      *[pltpu.with_memory_space_constraint(a, pltpu.HBM) for a in outside], *after)


def prepare(decay_ref, start_ref, rows_ref, cols_ref):
    tri = (
        lax.broadcasted_iota(jnp.int32, (BLOCK, BLOCK), 0) <= lax.broadcasted_iota(jnp.int32, (BLOCK, BLOCK), 1)
    ).astype(F32)
    for b in range(decay_ref.shape[1] // BLOCK):
        at = block(b)
        starts = jnp.broadcast_to(start_ref[:, at].astype(F32), (8, BLOCK))
        both = jnp.concatenate([decay_ref[:, at], starts], axis=0)
        sums = lax.dot_general(both, tri, NN, precision=lax.Precision.HIGHEST, preferred_element_type=F32)
        cumul, marks = sums[:8], sums[8:]
        last, last_mark = cumul[:, BLOCK - 1 :], marks[:, BLOCK - 1 :]
        entering = jnp.where(marks == 0.0, jnp.exp(cumul), 0.0)
        leaving = jnp.where(marks == last_mark, jnp.exp(last - cumul), 0.0)
        stack = jnp.concatenate([cumul, entering, leaving, marks], axis=0)
        rows_ref[:, at] = stack
        cols_ref[at, :] = jnp.concatenate([stack, jnp.zeros((96, BLOCK), F32)], axis=0).T


def keeps(rows_ref, head):
    enter = rows_ref[8 + head : 9 + head, :]
    k0 = jnp.broadcast_to(enter[:, BLOCK - 1 : BLOCK], (1, DH))
    k1 = jnp.broadcast_to(enter[:, 2 * BLOCK - 1 : 2 * BLOCK], (1, DH))
    return k0, k1


def send_out(place, k, terms_ref, keep_ref, own_ref, send_ref):
    for out, first in ((own_ref, 0), (send_ref, 2 * k)):
        for r in range(2 * k):
            group, j = (first + r) // k, (first + r) % k
            head = (group ^ group_of(place)) * k + j
            out[cut(r), :] = terms_ref[head]
            out[pl.ds(2 * k * DH + r, 1), :] = keep_ref[pl.ds(head, 1), :]
        rest = 8 - 2 * k
        out[2 * k * DH + 2 * k :, :] = jnp.ones((rest, DH), F32)


def turned_half(place, k, i):
    return ((i // k) ^ ((place[0] >> 1) & 1)) * k + i % k


def at_rows(i):
    return pl.ds(pl.multiple_of(i * DH, DH), DH)


def each_half(place, other, work):
    for p in range(2):
        pl.when(((place[0] & 1) ^ other) == p)(functools.partial(work, p))


def k1_body(k, head0, chunks, place, *refs):
    heads = GROUPS * k
    if head0 == 0:
        decay_hbm, start_hbm, key_hbm, value_hbm, own_ref, send_ref, loc_ref, rows_ref, cols_ref = refs[:9]
        copied = refs[9 : 9 + 2 * chunks]
        terms_ref, keep_ref, decay_ref, start_ref, sems = refs[9 + 2 * chunks :]
        loads = [
            pltpu.make_async_copy(decay_hbm, decay_ref, sems.at[0]),
            pltpu.make_async_copy(start_hbm, start_ref, sems.at[1]),
        ]
        for n, target in enumerate(copied):
            source, first = (key_hbm, value_hbm)[n % 2], n // 2 * heads * DH
            loads.append(pltpu.make_async_copy(source.at[:, first : first + heads * DH], target, sems.at[2 + n]))
        for load in loads:
            load.start()
        loads[0].wait()
        loads[1].wait()
        prepare(decay_ref, start_ref, rows_ref, cols_ref)
        loads[2].wait()
        loads[3].wait()
        key_ref, value_ref = copied[:2]
    else:
        rows_ref, key_ref, value_ref, own_ref, send_ref, loc_ref, terms_ref, keep_ref = refs
        loads = []
    for j in range(heads):
        head = head0 + j
        leave = rows_ref[16 + head : 17 + head, :]
        terms = []
        for b in range(2):
            keys = key_ref[block(b), cut(j)].T.astype(F32)
            scaled = (keys * leave[:, block(b)]).astype(BF16)
            terms.append(mm(scaled, value_ref[block(b), cut(j)]))
        k0, k1 = keeps(rows_ref, head)
        loc_ref[j] = terms[0]
        terms_ref[j] = k1 * terms[0] + terms[1]
        keep_ref[j : j + 1, :] = k0 * k1
    send_out(place, k, terms_ref, keep_ref, own_ref, send_ref)
    for load in loads[4:]:
        load.wait()


def make_bias(rows_ref, cols_ref, bias_ref, turned_ref):
    down = lax.broadcasted_iota(jnp.int32, (BLOCK, BLOCK), 0)
    along = lax.broadcasted_iota(jnp.int32, (BLOCK, BLOCK), 1)
    for b in range(2):
        same = cols_ref[block(b), 24:25] == rows_ref[24:25, block(b)]
        bias_ref[b] = jnp.where((down >= along) & same, 0.0, FAR)
        turned_ref[b] = jnp.where((down <= along) & same, 0.0, FAR)


def k2_body(first, head0, base, count, place, query_ref, key_ref, value_ref, rows_ref, cols_ref, *refs):
    if first:
        (within_ref, grid_ref, turned_ref, weighted_ref, scaled_ref, enter_ref, leave_ref,
         bias_ref, bias_turned_ref) = refs
        make_bias(rows_ref, cols_ref, bias_ref, bias_turned_ref)
    else:
        (bias_ref, bias_turned_ref, within_ref, grid_ref, turned_ref, weighted_ref, scaled_ref, enter_ref,
         leave_ref) = refs
    zeros = jnp.zeros((HALF, HALF), F32)
    for j in range(count):
        head = head0 + j
        inner = head - base
        for b in range(2):
            at = block(b)
            query, key = query_ref[at, cut(head)], key_ref[at, cut(inner)]
            cum_row = rows_ref[head : head + 1, at]
            top, low = slice(0, HALF), slice(HALF, BLOCK)
            cum_top = jnp.broadcast_to(cols_ref[b * BLOCK : b * BLOCK + HALF, head : head + 1], (HALF, HALF))
            cum_low = jnp.broadcast_to(cols_ref[b * BLOCK + HALF : (b + 1) * BLOCK, head : head + 1], (HALF, HALF))
            row_top, row_low = cum_row[:, :HALF], cum_row[:, HALF:]

            def decay(difference, limit):
                return jnp.exp(jnp.minimum(difference, limit))

            grid_ref[j, b, top, top] = decay(cum_top - row_top, bias_ref[b, top, top])
            grid_ref[j, b, low, top] = decay(cum_low - row_top, bias_ref[b, low, top])
            grid_ref[j, b, low, low] = decay(cum_low - row_low, bias_ref[b, low, low])
            grid_ref[j, b, top, low] = zeros
            turned_ref[j, b, top, top] = decay(row_top - cum_top, bias_turned_ref[b, top, top])
            turned_ref[j, b, top, low] = decay(row_low - cum_top, bias_turned_ref[b, top, low])
            turned_ref[j, b, low, low] = decay(row_low - cum_low, bias_turned_ref[b, low, low])
            turned_ref[j, b, low, top] = zeros
            weighted = (mm(query, key, NT) * grid_ref[j, b]).astype(BF16)
            weighted_ref[j, b] = (mm(key, query, NT) * turned_ref[j, b]).astype(BF16)
            within_ref[at, cut(j)] = mm(weighted, value_ref[at, cut(inner)])
            enter = rows_ref[8 + head : 9 + head, at]
            scaled_ref[j, b] = (query.T.astype(F32) * enter).astype(BF16)
            enter_ref[at, cut(j)] = jnp.broadcast_to(cols_ref[at, 8 + head : 9 + head], (BLOCK, DH))
            leave_ref[at, cut(j)] = jnp.broadcast_to(cols_ref[at, 16 + head : 17 + head], (BLOCK, DH))


def k3_body(k, head0, other, place, query_ref, grad_ref, loc_ref, rows_ref, state_ref, *refs):
    per = 2 * k
    withins, scaleds, enters, refs = refs[:2], refs[2:4], refs[4:6], refs[6:]
    message_ref, mixgrad_ref, states_ref, back_ref, attended_ref = refs[-5:]
    message_ref[per * DH :, :] = jnp.ones((8, DH), F32)

    def work(p):
        for i in range(per):
            j = p * per + i
            head = head0 + j
            stand = turned_half(place, k, i)
            k0, k1 = keeps(rows_ref, head)
            incoming = state_ref[at_rows(stand), :]
            states = (incoming, k0 * incoming + loc_ref[j])
            backs = []
            for b in range(2):
                at = block(b)
                low = states[b].astype(BF16)
                states_ref[j, b] = low
                mixture = withins[p][at, cut(i)] + mm(query_ref[at, cut(head)], low) * enters[p][at, cut(i)]
                wide = grad_ref[at, cut(head)].astype(F32)
                inverse = lax.rsqrt(jnp.mean(mixture * mixture, axis=1, keepdims=True) + EPS)
                along = jnp.mean(wide * mixture, axis=1, keepdims=True) * inverse
                normed = mixture * inverse
                attended_ref[at, cut(j)] = normed.astype(BF16)
                mixgrad = (inverse * (wide - normed * along)).astype(BF16)
                mixgrad_ref[at, cut(j)] = mixgrad
                backs.append(mm(scaleds[p][i, b], mixgrad))
            back_ref[j] = backs[1]
            message_ref[at_rows(stand), :] = k0 * backs[1] + backs[0]
            message_ref[pl.ds(per * DH + stand, 1), :] = k0 * k1

    each_half(place, other, work)


def columns(ref, first, count):
    return ref.at[:, first * DH : (first + count) * DH]


def k4_body(head0, base, count, place, query_ref, key_ref, value_ref, mixgrad_ref, attended_ref, grid_ref,
            turned_ref, weighted_ref, states_ref, enter_ref, *refs):
    later = head0 > 0
    key_part_ref, value_part_ref, query_grad_ref, attended_hbm, query_grad_hbm, sems = refs[3 * later :]
    inner0 = head0 - base
    copies = [
        pltpu.make_async_copy(
            columns(attended_ref, inner0, count), columns(attended_hbm, head0, count), sems.at[0]
        )
    ]
    if later:
        copies.append(
            pltpu.make_async_copy(refs[0], columns(query_grad_hbm, head0 - count, count), sems.at[1])
        )
    for copy in copies:
        copy.start()
    for j in range(count):
        head = head0 + j
        inner = head - base
        for b in range(2):
            at = block(b)
            mixgrad = mixgrad_ref[at, cut(inner)]
            value = value_ref[at, cut(inner)]
            masked = (mm(mixgrad, value, NT) * grid_ref[j, b]).astype(BF16)
            query_grad_ref[at, cut(j)] = (
                mm(masked, key_ref[at, cut(inner)]) + mm(mixgrad, states_ref[inner, b], NT) * enter_ref[at, cut(j)]
            ).astype(BF16)
            turned = (mm(value, mixgrad, NT) * turned_ref[j, b]).astype(BF16)
            key_part_ref[at, cut(j)] = mm(turned, query_ref[at, cut(head)])
            value_part_ref[at, cut(j)] = mm(weighted_ref[j, b], mixgrad)
    for copy in copies:
        copy.wait()


def k5_body(k, head0, other, kept, query_at, place, key_ref, value_ref, back_ref, rows_ref, state_ref, *refs):
    per = 2 * k
    key_parts, value_parts, leaves, refs = refs[:2], refs[2:4], refs[4:6], refs[6:]
    left, refs = refs[: 2 * len(kept)], refs[2 * len(kept) :]
    if query_at is not None:
        query_ref, _, key_grad_ref, value_grad_ref, query_hbm, sems = refs
    elif kept:
        key_hbm, value_hbm, key_grad_ref, value_grad_ref, sems = refs
    else:
        key_grad_ref, value_grad_ref = refs

    def ship(source, target, sem):
        copy = pltpu.make_async_copy(source, target, sems.at[sem])
        copy.start()
        return copy

    copies = []
    if query_at is not None:
        copies.append(ship(query_ref, columns(query_hbm, query_at, per), 0))
    for n, (base, half) in enumerate(kept):
        start = pl.multiple_of((base + ((place[0] & 1) ^ half) * per) * DH, DH)
        copies.append(ship(left[2 * n], key_hbm.at[:, pl.ds(start, per * DH)], 2 * n))
        copies.append(ship(left[2 * n + 1], value_hbm.at[:, pl.ds(start, per * DH)], 2 * n + 1))

    def work(p):
        ours = []
        for i in range(per):
            j = p * per + i
            k0, k1 = keeps(rows_ref, head0 + j)
            outgoing = state_ref[at_rows(turned_half(place, k, i)), :]
            afters = (k1 * outgoing + back_ref[j], outgoing)
            for b in range(2):
                at = block(b)
                low = afters[b].astype(BF16)
                leave = leaves[p][at, cut(i)]
                key_grad_ref[at, cut(i)] = (
                    key_parts[p][at, cut(i)] + mm(value_ref[at, cut(j)], low, NT) * leave
                ).astype(BF16)
                value_grad_ref[at, cut(i)] = (
                    value_parts[p][at, cut(i)] + mm(key_ref[at, cut(j)], low) * leave
                ).astype(BF16)
            if kept:
                sem = 2 * len(kept) + 2 * i
                ours.append(ship(columns(key_grad_ref, i, 1), columns(key_hbm, head0 + j, 1), sem))
                ours.append(ship(columns(value_grad_ref, i, 1), columns(value_hbm, head0 + j, 1), sem + 1))
        for copy in ours:
            copy.wait()

    each_half(place, other, work)
    for copy in copies:
        copy.wait()


def joined(later, got_ref, held_ref, heads, j):
    one = slice(heads * DH + j, heads * DH + j + 1)
    a_got, a_held = got_ref[one, :], held_ref[one, :]
    state = jnp.where(later, a_held, 1.0) * got_ref[cut(j), :] + jnp.where(later, 1.0, a_got) * held_ref[cut(j), :]
    return state, a_got * a_held


def before(later, got_ref, prefix_ref, k, j):
    one = slice(k * DH + j, k * DH + j + 1)
    a_got = got_ref[one, :]
    if prefix_ref is None:
        return jnp.where(later, 1.0, 0.0) * got_ref[cut(j), :], jnp.where(later, a_got, 1.0)
    a = prefix_ref[one, :]
    state = jnp.where(later, a, 0.0) * got_ref[cut(j), :] + prefix_ref[cut(j), :]
    return state, jnp.where(later, a * a_got, a)


def put(out, heads, j, value):
    out[cut(j), :], out[heads * DH + j : heads * DH + j + 1, :] = value


def c1_body(turn, k, place, own_ref, got_ref, keep_ref, send_ref):
    later = (position(place, turn) & 1) == 1
    for out in (keep_ref, send_ref):
        out[k * DH :, :] = jnp.ones((8, DH), F32)
    for j in range(2 * k):
        put(keep_ref if j < k else send_ref, k, j % k, joined(later, got_ref, own_ref, 2 * k, j))


def c2_body(turn, k, place, own_ref, got_ref, total_ref):
    later = (position(place, turn) & 2) == 2
    total_ref[k * DH :, :] = jnp.ones((8, DH), F32)
    for j in range(k):
        put(total_ref, k, j, joined(later, got_ref, own_ref, k, j))


def cz_body(turn, k, bit, first, place, *refs):
    total_ref, got_ref = refs[:2]
    prefix_ref = None if first else refs[2]
    new_total_ref, new_prefix_ref = refs[-2:]
    later = (position(place, turn) & bit) == bit
    for out in (new_total_ref, new_prefix_ref):
        out[k * DH :, :] = jnp.ones((8, DH), F32)
    for j in range(k):
        put(new_total_ref, k, j, joined(later, got_ref, total_ref, k, j))
        put(new_prefix_ref, k, j, before(later, got_ref, prefix_ref, k, j))


def c3_body(turn, k, bit, first, place, *refs):
    got_ref = refs[0]
    prefix_ref = None if first else refs[1]
    own_ref, chip_ref, mine_ref, send_ref = refs[-4:]
    later = (position(place, turn) & bit) == bit
    upper = (position(place, turn) & 2) == 2
    for j in range(k):
        at, one = cut(j), slice(k * DH + j, k * DH + j + 1)
        prefix, _ = before(later, got_ref, prefix_ref, k, j)
        mine_ref[at, :] = jnp.where(upper, chip_ref[one, :], 1.0) * prefix + jnp.where(upper, 1.0, 0.0) * chip_ref[at, :]
        send_ref[at, :] = jnp.where(upper, 1.0, own_ref[one, :]) * prefix + jnp.where(upper, 0.0, 1.0) * own_ref[at, :]


def c4_body(turn, k, place, half_ref, got_half_ref, own_ref, got_ref, mine_ref, send_ref):
    later = (position(place, turn) & 1) == 1
    for j in range(2 * k):
        at, one = cut(j), slice(2 * k * DH + j, 2 * k * DH + j + 1)
        chip = half_ref[cut(j), :] if j < k else got_half_ref[cut(j - k), :]
        mine_ref[at, :] = jnp.where(later, got_ref[one, :], 1.0) * chip + jnp.where(later, 1.0, 0.0) * got_ref[at, :]
        send_ref[at, :] = jnp.where(later, 1.0, own_ref[one, :]) * chip + jnp.where(later, 0.0, 1.0) * own_ref[at, :]


def exchange(x, bit, count):
    return lax.ppermute(x, "seq", [(i, i ^ bit) for i in range(count)])


class Order:
    def __init__(self, place):
        self.place, self.last = place, ()

    def __call__(self, body, inside, outs, **options):
        taken = [id(a) for a in (*options.get("outside", ()), *inside)]
        after = tuple(a for a in self.last if id(a) not in taken)
        out = run(body, self.place, inside, outs, after=after, **options)
        self.last = (out[0],)
        return out


def scan_devices(call, own, send, turn, k, count):
    half = ((k * DH + 8, DH), F32)
    got = exchange(send, 1, count)
    yield
    own = own()
    chip, chip_send = call(functools.partial(c1_body, turn, k), (own, got), (half, half))
    chip_got = exchange(chip_send, 2, count)
    yield
    (total,) = call(functools.partial(c2_body, turn, k), (chip, chip_got), (half,))
    prefix = ()
    bit = 4
    while bit < count:
        got_total = exchange(total, bit, count)
        yield
        if bit * 2 < count:
            body = functools.partial(cz_body, turn, k, bit, not prefix)
            total, *prefix = call(body, (total, got_total, *prefix), (half, half))
        else:
            body = functools.partial(c3_body, turn, k, bit, not prefix)
            mine, mine_send = call(body, (got_total, *prefix, chip, chip_got), (((k * DH, DH), F32),) * 2)
        bit *= 2
    mine_got = exchange(mine_send, 2, count)
    yield
    body = functools.partial(c4_body, turn, k)
    state, state_send = call(body, (mine, mine_got, own, got), (((2 * k * DH, DH), F32),) * 2)
    yield state, exchange(state_send, 1, count)


def drive(scans, fillers, rounds, late=None):
    fillers = list(fillers)
    for step in range(rounds):
        for c, scan in enumerate(scans):
            if step == 1 and late:
                late(c)
            next(scan)
        if step and fillers:
            fillers.pop(0)()
    for filler in fillers:
        filler()


def by_halves(scans, half, turns):
    ready = {}
    for c, other in turns:
        for n in range(c + 1 + (len(ready) > 0 and c + 1 < len(scans))):
            if n not in ready:
                ready[n] = next(scans[n])
        half(c, other, ready[c][other])
    return ready


def local(query_rows, key_rows, value_rows, log_decay, run_start, out_grad):
    all_heads = log_decay.shape[0]
    tokens, width = query_rows.shape
    count = lax.axis_size("seq")
    seat = lax.axis_index("seq")
    call = Order(seat.reshape(1))
    heads = all_heads // CHUNKS
    k = heads // GROUPS
    per = heads // PIECES
    chunks = range(CHUNKS)
    dma = pltpu.SemaphoreType.DMA
    message = ((2 * k * DH + 8, DH), F32)
    states = ((heads, DH, DH), F32)
    flat = jax.ShapeDtypeStruct((tokens, width), BF16)
    chunk_bf16 = ((tokens, heads * DH), BF16)
    piece_f32 = ((tokens, per * DH), F32)
    half_bf16 = ((tokens, per * DH), BF16)
    square = (per, 2, BLOCK, BLOCK)
    mask = ((2, BLOCK, BLOCK), F32)
    scratch_terms = (pltpu.VMEM((heads, DH, DH), F32), pltpu.VMEM((8, DH), F32))

    loc, scans = [], []
    for c in chunks:
        outs = (message, message, states)
        scratch = scratch_terms
        body = functools.partial(k1_body, k, c * heads, CHUNKS)
        if c == 0:
            outs += (((32, tokens), F32), ((tokens, DH), F32)) + (chunk_bf16,) * (2 * CHUNKS)
            scratch += (pltpu.VMEM(log_decay.shape, F32), pltpu.VMEM((1, tokens), jnp.int32), dma((2 * CHUNKS + 2,)))
            outside = (log_decay, run_start.reshape(1, tokens), key_rows, value_rows)
            out = call(body, (), outs, outside=outside, scratch=scratch)
            rows, cols = out[3:5]
            keys, values = out[5::2], out[6::2]
        else:
            out = call(body, (rows, keys[c], values[c]), outs, scratch=scratch)
        loc.append(out[2])
        scans.append(scan_devices(call, lambda own=out[0]: own, out[1], False, k, count))

    forward = []

    def k2(n):
        c = n // PIECES
        outs = (piece_f32, (square, F32), (square, F32), (square, BF16), ((per, 2, DH, BLOCK), BF16))
        outs += (piece_f32, piece_f32)
        inputs = (query_rows, keys[c], values[c], rows, cols)
        if n == 0:
            outs += (mask, mask)
        else:
            inputs += tuple(forward[0][7:])
        forward.append(call(functools.partial(k2_body, n == 0, n * per, c * heads, per), inputs, outs))

    fillers = range(CHUNKS * PIECES)
    rounds = count.bit_length()
    drive(scans, [functools.partial(k2, n) for n in fillers], rounds)
    middle, newest = {}, {}

    def k3(c, other, state):
        mid = forward[c * PIECES : (c + 1) * PIECES]
        inside = (query_rows, out_grad, loc[c], rows, state)
        inside += tuple(f[i] for i in (0, 4, 5) for f in mid)
        renewed = {len(inside) + i: 1 + i for i in range(4)} if c in newest else None
        out = call(
            functools.partial(k3_body, k, c * heads, other),
            inside + tuple(newest.get(c, ())),
            (message, chunk_bf16, ((heads, 2, DH, DH), BF16), states, chunk_bf16),
            renewed=renewed,
        )
        middle[c, other], newest[c] = out[0], out[1:]

    ready = by_halves(scans, k3, K3_TURNS)
    late = {c for c in chunks if (c, 0) not in K3_TURNS}
    scans = [scan_devices(call, lambda c=c: middle[c, 0], middle[c, 1], True, k, count) for c in chunks]

    backward = []

    def k4(n):
        c = n // PIECES
        mixgrad, states_low, _, attended = newest[c]
        f = forward[n]
        backward.append(
            call(
                functools.partial(k4_body, n * per, c * heads, per),
                (query_rows, keys[c], values[c], mixgrad, attended, f[1], f[2], f[3], states_low, f[5])
                + ((backward[-1][2],) if n else ()),
                (piece_f32, piece_f32, ((tokens, per * DH), BF16), flat, flat),
                outside=tuple(backward[-1][3:]) if n else (),
                aliases={0: 3, 1: 4} if n else None,
                scratch=(dma((2,)),),
            )
        )

    drive(scans, [functools.partial(k4, n) for n in fillers], rounds, lambda c: k3(c, 0, ready[c][0]) if c in late else None)
    attended, query_grad = backward[-1][3:]
    final = []

    def k5(c, other, state):
        last = c == CHUNKS - 1 and other == 1
        mid = [forward[n] for n in range(c * PIECES, (c + 1) * PIECES)]
        back = [backward[n] for n in range(c * PIECES, (c + 1) * PIECES)]
        inside = (keys[c], values[c], newest[c][2], rows, state)
        inside += tuple(b[0] for b in back) + tuple(b[1] for b in back) + tuple(f[6] for f in mid)
        kept, query_at, options = (), None, {}
        outs = (half_bf16, half_bf16)
        if not final:
            inside += (backward[-1][2],)
            query_at = CHUNKS * heads - per
            outs += (flat,)
            options = {"outside": (query_grad,), "aliases": {0: 2}, "scratch": (dma((1,)),)}
        elif last:
            kept = tuple(f[1:] for f in final)
            inside += tuple(a for f in final for a in f[0][:2])
            outs = (flat, flat)
            half = pltpu.VMEM((tokens, per * DH), BF16)
            options = {"scratch": (half, half, dma((2 * len(kept) + 2 * per,)))}
        body = functools.partial(k5_body, k, c * heads, other, kept, query_at)
        final.append((call(body, inside, outs, **options), c * heads, other))

    by_halves(scans, k5, K5_TURNS)
    return attended, final[0][0][2], *final[-1][0]


def solution(mesh):
    rows = P(("groups", "seq"), None)
    return jax.shard_map(
        local,
        mesh=mesh,
        in_specs=(rows, rows, rows, P(None, ("groups", "seq")), P(("groups", "seq")), rows),
        out_specs=(rows, rows, rows, rows),
        check_vma=False,
    )
```

```python
import functools

import jax
import jax.numpy as jnp
from jax import lax
from jax.experimental import pallas as pl
from jax.experimental.pallas import tpu as pltpu
from jax.sharding import PartitionSpec as P

BLOCK = 256
HALF = 128
DH = 128
EPS = 1e-05
FAR = -1e30
GROUPS = 4
CHUNKS = 2
K3_TURNS = ((0, 0), (0, 1), (1, 1))
K5_TURNS = ((0, 0), (0, 1), (1, 0), (1, 1))
PIECES = 2
F32 = jnp.float32
BF16 = jnp.bfloat16

NN = (((1,), (0,)), ((), ()))
NT = (((1,), (1,)), ((), ()))
TN = (((0,), (0,)), ((), ()))


def mm(a, b, dims=NN):
    return lax.dot_general(a, b, dims, preferred_element_type=F32)


def cut(j):
    return slice(j * DH, (j + 1) * DH)


def block(b):
    return slice(b * BLOCK, (b + 1) * BLOCK)


def group_of(place):
    return ((place[0] & 1) << 1) | ((place[0] >> 1) & 1)


def position(place, backward):
    return ~place[0] if backward else place[0]


SMEM = pl.BlockSpec(memory_space=pltpu.SMEM)
VMEM = pl.BlockSpec(memory_space=pltpu.VMEM)
ANY = pl.BlockSpec(memory_space=pl.ANY)
HBM = pl.BlockSpec(memory_space=pltpu.HBM)


def run(body, scalar, inside, outs, outside=(), after=(), aliases=None, renewed=None, scratch=(), megabytes=8):
    taken = len(inside) + len(outside)

    def kernel(scalar_ref, *refs):
        body(scalar_ref, *refs[:taken], *refs[taken + len(after) :])

    shapes = [pltpu.HBM(o.shape, o.dtype) if isinstance(o, jax.ShapeDtypeStruct) else pltpu.VMEM(*o) for o in outs]
    return pl.pallas_call(
        kernel,
        in_specs=[SMEM] + [VMEM] * len(inside) + [HBM] * len(outside) + [ANY] * len(after),
        out_specs=[HBM if isinstance(o, jax.ShapeDtypeStruct) else VMEM for o in outs],
        out_shape=shapes,
        input_output_aliases={1 + len(inside) + i: o for i, o in (aliases or {}).items()}
        | {1 + i: o for i, o in (renewed or {}).items()},
        scratch_shapes=list(scratch),
        compiler_params=pltpu.CompilerParams(vmem_limit_bytes=megabytes << 20),
    )(scalar, *[pltpu.with_memory_space_constraint(a, pltpu.VMEM) for a in inside],
      *[pltpu.with_memory_space_constraint(a, pltpu.HBM) for a in outside], *after)


def prepare(decay_ref, start_ref, rows_ref, cols_ref):
    tri = (
        lax.broadcasted_iota(jnp.int32, (BLOCK, BLOCK), 0) <= lax.broadcasted_iota(jnp.int32, (BLOCK, BLOCK), 1)
    ).astype(F32)
    for b in range(decay_ref.shape[1] // BLOCK):
        at = block(b)
        starts = jnp.broadcast_to(start_ref[:, at].astype(F32), (8, BLOCK))
        both = jnp.concatenate([decay_ref[:, at], starts], axis=0)
        sums = lax.dot_general(both, tri, NN, precision=lax.Precision.HIGHEST, preferred_element_type=F32)
        cumul, marks = sums[:8], sums[8:]
        last, last_mark = cumul[:, BLOCK - 1 :], marks[:, BLOCK - 1 :]
        entering = jnp.where(marks == 0.0, jnp.exp(cumul), 0.0)
        leaving = jnp.where(marks == last_mark, jnp.exp(last - cumul), 0.0)
        stack = jnp.concatenate([cumul, entering, leaving, marks], axis=0)
        rows_ref[:, at] = stack
        cols_ref[at, :] = jnp.concatenate([stack, jnp.zeros((96, BLOCK), F32)], axis=0).T


def keeps(rows_ref, head):
    enter = rows_ref[8 + head : 9 + head, :]
    k0 = jnp.broadcast_to(enter[:, BLOCK - 1 : BLOCK], (1, DH))
    k1 = jnp.broadcast_to(enter[:, 2 * BLOCK - 1 : 2 * BLOCK], (1, DH))
    return k0, k1


def send_out(place, k, terms_ref, keep_ref, own_ref, send_ref):
    for out, first in ((own_ref, 0), (send_ref, 2 * k)):
        for r in range(2 * k):
            group, j = (first + r) // k, (first + r) % k
            head = (group ^ group_of(place)) * k + j
            out[cut(r), :] = terms_ref[head]
            out[pl.ds(2 * k * DH + r, 1), :] = keep_ref[pl.ds(head, 1), :]
        rest = 8 - 2 * k
        out[2 * k * DH + 2 * k :, :] = jnp.ones((rest, DH), F32)


def turned_half(place, k, i):
    return ((i // k) ^ ((place[0] >> 1) & 1)) * k + i % k


def at_rows(i):
    return pl.ds(pl.multiple_of(i * DH, DH), DH)


def each_half(place, other, work):
    for p in range(2):
        pl.when(((place[0] & 1) ^ other) == p)(functools.partial(work, p))


def k1_body(k, head0, chunks, place, *refs):
    heads = GROUPS * k
    if head0 == 0:
        decay_hbm, start_hbm, key_hbm, value_hbm, own_ref, send_ref, loc_ref, rows_ref, cols_ref = refs[:9]
        copied = refs[9 : 9 + 2 * chunks]
        terms_ref, keep_ref, decay_ref, start_ref, sems = refs[9 + 2 * chunks :]
        loads = [
            pltpu.make_async_copy(decay_hbm, decay_ref, sems.at[0]),
            pltpu.make_async_copy(start_hbm, start_ref, sems.at[1]),
        ]
        for n, target in enumerate(copied):
            source, first = (key_hbm, value_hbm)[n % 2], n // 2 * heads * DH
            loads.append(pltpu.make_async_copy(source.at[:, first : first + heads * DH], target, sems.at[2 + n]))
        for load in loads:
            load.start()
        loads[0].wait()
        loads[1].wait()
        prepare(decay_ref, start_ref, rows_ref, cols_ref)
        loads[2].wait()
        loads[3].wait()
        key_ref, value_ref = copied[:2]
    else:
        rows_ref, key_ref, value_ref, own_ref, send_ref, loc_ref, terms_ref, keep_ref = refs
        loads = []
    for j in range(heads):
        head = head0 + j
        leave = rows_ref[16 + head : 17 + head, :]
        terms = []
        for b in range(2):
            keys = key_ref[block(b), cut(j)].T.astype(F32)
            scaled = (keys * leave[:, block(b)]).astype(BF16)
            terms.append(mm(scaled, value_ref[block(b), cut(j)]))
        k0, k1 = keeps(rows_ref, head)
        loc_ref[j] = terms[0]
        terms_ref[j] = k1 * terms[0] + terms[1]
        keep_ref[j : j + 1, :] = k0 * k1
    send_out(place, k, terms_ref, keep_ref, own_ref, send_ref)
    for load in loads[4:]:
        load.wait()


def make_bias(rows_ref, cols_ref, bias_ref, turned_ref):
    down = lax.broadcasted_iota(jnp.int32, (BLOCK, BLOCK), 0)
    along = lax.broadcasted_iota(jnp.int32, (BLOCK, BLOCK), 1)
    for b in range(2):
        same = cols_ref[block(b), 24:25] == rows_ref[24:25, block(b)]
        bias_ref[b] = jnp.where((down >= along) & same, 0.0, FAR)
        turned_ref[b] = jnp.where((down <= along) & same, 0.0, FAR)


def k2_body(first, head0, base, count, place, query_ref, key_ref, value_ref, rows_ref, cols_ref, *refs):
    if first:
        (within_ref, grid_ref, turned_ref, weighted_ref, scaled_ref, enter_ref, leave_ref,
         bias_ref, bias_turned_ref) = refs
        make_bias(rows_ref, cols_ref, bias_ref, bias_turned_ref)
    else:
        (bias_ref, bias_turned_ref, within_ref, grid_ref, turned_ref, weighted_ref, scaled_ref, enter_ref,
         leave_ref) = refs
    zeros = jnp.zeros((HALF, HALF), F32)
    for j in range(count):
        head = head0 + j
        inner = head - base
        for b in range(2):
            at = block(b)
            query, key = query_ref[at, cut(head)], key_ref[at, cut(inner)]
            cum_row = rows_ref[head : head + 1, at]
            top, low = slice(0, HALF), slice(HALF, BLOCK)
            cum_top = jnp.broadcast_to(cols_ref[b * BLOCK : b * BLOCK + HALF, head : head + 1], (HALF, HALF))
            cum_low = jnp.broadcast_to(cols_ref[b * BLOCK + HALF : (b + 1) * BLOCK, head : head + 1], (HALF, HALF))
            row_top, row_low = cum_row[:, :HALF], cum_row[:, HALF:]

            def decay(difference, limit):
                return jnp.exp(jnp.minimum(difference, limit))

            grid_ref[j, b, top, top] = decay(cum_top - row_top, bias_ref[b, top, top])
            grid_ref[j, b, low, top] = decay(cum_low - row_top, bias_ref[b, low, top])
            grid_ref[j, b, low, low] = decay(cum_low - row_low, bias_ref[b, low, low])
            grid_ref[j, b, top, low] = zeros
            turned_ref[j, b, top, top] = decay(row_top - cum_top, bias_turned_ref[b, top, top])
            turned_ref[j, b, top, low] = decay(row_low - cum_top, bias_turned_ref[b, top, low])
            turned_ref[j, b, low, low] = decay(row_low - cum_low, bias_turned_ref[b, low, low])
            turned_ref[j, b, low, top] = zeros
            weighted = (mm(query, key, NT) * grid_ref[j, b]).astype(BF16)
            weighted_ref[j, b] = (mm(key, query, NT) * turned_ref[j, b]).astype(BF16)
            within_ref[at, cut(j)] = mm(weighted, value_ref[at, cut(inner)])
            enter = rows_ref[8 + head : 9 + head, at]
            scaled_ref[j, b] = (query.T.astype(F32) * enter).astype(BF16)
            enter_ref[at, cut(j)] = jnp.broadcast_to(cols_ref[at, 8 + head : 9 + head], (BLOCK, DH))
            leave_ref[at, cut(j)] = jnp.broadcast_to(cols_ref[at, 16 + head : 17 + head], (BLOCK, DH))


def k3_body(k, head0, other, place, query_ref, grad_ref, loc_ref, rows_ref, state_ref, *refs):
    per = 2 * k
    withins, scaleds, enters, refs = refs[:2], refs[2:4], refs[4:6], refs[6:]
    message_ref, mixgrad_ref, states_ref, back_ref, attended_ref = refs[-5:]
    message_ref[per * DH :, :] = jnp.ones((8, DH), F32)

    def work(p):
        for i in range(per):
            j = p * per + i
            head = head0 + j
            stand = turned_half(place, k, i)
            k0, k1 = keeps(rows_ref, head)
            incoming = state_ref[at_rows(stand), :]
            states = (incoming, k0 * incoming + loc_ref[j])
            backs = []
            for b in range(2):
                at = block(b)
                low = states[b].astype(BF16)
                states_ref[j, b] = low
                mixture = withins[p][at, cut(i)] + mm(query_ref[at, cut(head)], low) * enters[p][at, cut(i)]
                wide = grad_ref[at, cut(head)].astype(F32)
                inverse = lax.rsqrt(jnp.mean(mixture * mixture, axis=1, keepdims=True) + EPS)
                along = jnp.mean(wide * mixture, axis=1, keepdims=True) * inverse
                normed = mixture * inverse
                attended_ref[at, cut(j)] = normed.astype(BF16)
                mixgrad = (inverse * (wide - normed * along)).astype(BF16)
                mixgrad_ref[at, cut(j)] = mixgrad
                backs.append(mm(scaleds[p][i, b], mixgrad))
            back_ref[j] = backs[1]
            message_ref[at_rows(stand), :] = k0 * backs[1] + backs[0]
            message_ref[pl.ds(per * DH + stand, 1), :] = k0 * k1

    each_half(place, other, work)


def columns(ref, first, count):
    return ref.at[:, first * DH : (first + count) * DH]


def k4_body(head0, base, count, place, query_ref, key_ref, value_ref, mixgrad_ref, attended_ref, grid_ref,
            turned_ref, weighted_ref, states_ref, enter_ref, *refs):
    later = head0 > 0
    key_part_ref, value_part_ref, query_grad_ref, attended_hbm, query_grad_hbm, sems = refs[3 * later :]
    inner0 = head0 - base
    copies = [
        pltpu.make_async_copy(
            columns(attended_ref, inner0, count), columns(attended_hbm, head0, count), sems.at[0]
        )
    ]
    if later:
        copies.append(
            pltpu.make_async_copy(refs[0], columns(query_grad_hbm, head0 - count, count), sems.at[1])
        )
    for copy in copies:
        copy.start()
    for j in range(count):
        head = head0 + j
        inner = head - base
        for b in range(2):
            at = block(b)
            mixgrad = mixgrad_ref[at, cut(inner)]
            value = value_ref[at, cut(inner)]
            masked = (mm(mixgrad, value, NT) * grid_ref[j, b]).astype(BF16)
            query_grad_ref[at, cut(j)] = (
                mm(masked, key_ref[at, cut(inner)]) + mm(mixgrad, states_ref[inner, b], NT) * enter_ref[at, cut(j)]
            ).astype(BF16)
            turned = (mm(value, mixgrad, NT) * turned_ref[j, b]).astype(BF16)
            key_part_ref[at, cut(j)] = mm(turned, query_ref[at, cut(head)])
            value_part_ref[at, cut(j)] = mm(weighted_ref[j, b], mixgrad)
    for copy in copies:
        copy.wait()


def k5_body(k, head0, other, kept, query_at, place, key_ref, value_ref, back_ref, rows_ref, state_ref, *refs):
    per = 2 * k
    key_parts, value_parts, leaves, refs = refs[:2], refs[2:4], refs[4:6], refs[6:]
    left, refs = refs[: 2 * len(kept)], refs[2 * len(kept) :]
    if query_at is not None:
        query_ref, _, key_grad_ref, value_grad_ref, query_hbm, sems = refs
    elif kept:
        key_hbm, value_hbm, key_grad_ref, value_grad_ref, sems = refs
    else:
        key_grad_ref, value_grad_ref = refs

    def ship(source, target, sem):
        copy = pltpu.make_async_copy(source, target, sems.at[sem])
        copy.start()
        return copy

    copies = []
    if query_at is not None:
        copies.append(ship(query_ref, columns(query_hbm, query_at, per), 0))
    for n, (base, half) in enumerate(kept):
        start = pl.multiple_of((base + ((place[0] & 1) ^ half) * per) * DH, DH)
        copies.append(ship(left[2 * n], key_hbm.at[:, pl.ds(start, per * DH)], 2 * n))
        copies.append(ship(left[2 * n + 1], value_hbm.at[:, pl.ds(start, per * DH)], 2 * n + 1))

    def work(p):
        ours = []
        for i in range(per):
            j = p * per + i
            k0, k1 = keeps(rows_ref, head0 + j)
            outgoing = state_ref[at_rows(turned_half(place, k, i)), :]
            afters = (k1 * outgoing + back_ref[j], outgoing)
            for b in range(2):
                at = block(b)
                low = afters[b].astype(BF16)
                leave = leaves[p][at, cut(i)]
                key_grad_ref[at, cut(i)] = (
                    key_parts[p][at, cut(i)] + mm(value_ref[at, cut(j)], low, NT) * leave
                ).astype(BF16)
                value_grad_ref[at, cut(i)] = (
                    value_parts[p][at, cut(i)] + mm(key_ref[at, cut(j)], low) * leave
                ).astype(BF16)
            if kept:
                sem = 2 * len(kept) + 2 * i
                ours.append(ship(columns(key_grad_ref, i, 1), columns(key_hbm, head0 + j, 1), sem))
                ours.append(ship(columns(value_grad_ref, i, 1), columns(value_hbm, head0 + j, 1), sem + 1))
        for copy in ours:
            copy.wait()

    each_half(place, other, work)
    for copy in copies:
        copy.wait()


def joined(later, got_ref, held_ref, heads, j):
    one = slice(heads * DH + j, heads * DH + j + 1)
    a_got, a_held = got_ref[one, :], held_ref[one, :]
    state = jnp.where(later, a_held, 1.0) * got_ref[cut(j), :] + jnp.where(later, 1.0, a_got) * held_ref[cut(j), :]
    return state, a_got * a_held


def before(later, got_ref, prefix_ref, k, j):
    one = slice(k * DH + j, k * DH + j + 1)
    a_got = got_ref[one, :]
    if prefix_ref is None:
        return jnp.where(later, 1.0, 0.0) * got_ref[cut(j), :], jnp.where(later, a_got, 1.0)
    a = prefix_ref[one, :]
    state = jnp.where(later, a, 0.0) * got_ref[cut(j), :] + prefix_ref[cut(j), :]
    return state, jnp.where(later, a * a_got, a)


def put(out, heads, j, value):
    out[cut(j), :], out[heads * DH + j : heads * DH + j + 1, :] = value


def c1_body(turn, k, place, own_ref, got_ref, keep_ref, send_ref):
    later = (position(place, turn) & 1) == 1
    for out in (keep_ref, send_ref):
        out[k * DH :, :] = jnp.ones((8, DH), F32)
    for j in range(2 * k):
        put(keep_ref if j < k else send_ref, k, j % k, joined(later, got_ref, own_ref, 2 * k, j))


def c2_body(turn, k, place, own_ref, got_ref, total_ref):
    later = (position(place, turn) & 2) == 2
    total_ref[k * DH :, :] = jnp.ones((8, DH), F32)
    for j in range(k):
        put(total_ref, k, j, joined(later, got_ref, own_ref, k, j))


def cz_body(turn, k, bit, first, place, *refs):
    total_ref, got_ref = refs[:2]
    prefix_ref = None if first else refs[2]
    new_total_ref, new_prefix_ref = refs[-2:]
    later = (position(place, turn) & bit) == bit
    for out in (new_total_ref, new_prefix_ref):
        out[k * DH :, :] = jnp.ones((8, DH), F32)
    for j in range(k):
        put(new_total_ref, k, j, joined(later, got_ref, total_ref, k, j))
        put(new_prefix_ref, k, j, before(later, got_ref, prefix_ref, k, j))


def c3_body(turn, k, bit, first, place, *refs):
    got_ref = refs[0]
    prefix_ref = None if first else refs[1]
    own_ref, chip_ref, mine_ref, send_ref = refs[-4:]
    later = (position(place, turn) & bit) == bit
    upper = (position(place, turn) & 2) == 2
    for j in range(k):
        at, one = cut(j), slice(k * DH + j, k * DH + j + 1)
        prefix, _ = before(later, got_ref, prefix_ref, k, j)
        mine_ref[at, :] = jnp.where(upper, chip_ref[one, :], 1.0) * prefix + jnp.where(upper, 1.0, 0.0) * chip_ref[at, :]
        send_ref[at, :] = jnp.where(upper, 1.0, own_ref[one, :]) * prefix + jnp.where(upper, 0.0, 1.0) * own_ref[at, :]


def c4_body(turn, k, place, half_ref, got_half_ref, own_ref, got_ref, mine_ref, send_ref):
    later = (position(place, turn) & 1) == 1
    for j in range(2 * k):
        at, one = cut(j), slice(2 * k * DH + j, 2 * k * DH + j + 1)
        chip = half_ref[cut(j), :] if j < k else got_half_ref[cut(j - k), :]
        mine_ref[at, :] = jnp.where(later, got_ref[one, :], 1.0) * chip + jnp.where(later, 1.0, 0.0) * got_ref[at, :]
        send_ref[at, :] = jnp.where(later, 1.0, own_ref[one, :]) * chip + jnp.where(later, 0.0, 1.0) * own_ref[at, :]


def exchange(x, bit, count):
    return lax.ppermute(x, "seq", [(i, i ^ bit) for i in range(count)])


class Order:
    def __init__(self, place):
        self.place, self.last = place, ()

    def __call__(self, body, inside, outs, **options):
        taken = [id(a) for a in (*options.get("outside", ()), *inside)]
        after = tuple(a for a in self.last if id(a) not in taken)
        out = run(body, self.place, inside, outs, after=after, **options)
        self.last = (out[0],)
        return out


def scan_devices(call, own, send, turn, k, count):
    half = ((k * DH + 8, DH), F32)
    got = exchange(send, 1, count)
    yield
    own = own()
    chip, chip_send = call(functools.partial(c1_body, turn, k), (own, got), (half, half))
    chip_got = exchange(chip_send, 2, count)
    yield
    (total,) = call(functools.partial(c2_body, turn, k), (chip, chip_got), (half,))
    prefix = ()
    bit = 4
    while bit < count:
        got_total = exchange(total, bit, count)
        yield
        if bit * 2 < count:
            body = functools.partial(cz_body, turn, k, bit, not prefix)
            total, *prefix = call(body, (total, got_total, *prefix), (half, half))
        else:
            body = functools.partial(c3_body, turn, k, bit, not prefix)
            mine, mine_send = call(body, (got_total, *prefix, chip, chip_got), (((k * DH, DH), F32),) * 2)
        bit *= 2
    mine_got = exchange(mine_send, 2, count)
    yield
    body = functools.partial(c4_body, turn, k)
    state, state_send = call(body, (mine, mine_got, own, got), (((2 * k * DH, DH), F32),) * 2)
    yield state, exchange(state_send, 1, count)


def drive(scans, fillers, rounds, late=None):
    fillers = list(fillers)
    for step in range(rounds):
        for c, scan in enumerate(scans):
            if step == 1 and late:
                late(c)
            next(scan)
        pieces = int(step > 0) if late else (step > 1) + (step == rounds - 2)
        for _ in range(min(pieces, len(fillers))):
            fillers.pop(0)()
    for filler in fillers:
        filler()


def by_halves(scans, half, turns):
    ready = {}
    for c, other in turns:
        for n in range(c + 1 + (len(ready) > 0 and c + 1 < len(scans))):
            if n not in ready:
                ready[n] = next(scans[n])
        half(c, other, ready[c][other])
    return ready


def local(query_rows, key_rows, value_rows, log_decay, run_start, out_grad):
    all_heads = log_decay.shape[0]
    tokens, width = query_rows.shape
    count = lax.axis_size("seq")
    seat = lax.axis_index("seq")
    call = Order(seat.reshape(1))
    heads = all_heads // CHUNKS
    k = heads // GROUPS
    per = heads // PIECES
    chunks = range(CHUNKS)
    dma = pltpu.SemaphoreType.DMA
    message = ((2 * k * DH + 8, DH), F32)
    states = ((heads, DH, DH), F32)
    flat = jax.ShapeDtypeStruct((tokens, width), BF16)
    chunk_bf16 = ((tokens, heads * DH), BF16)
    piece_f32 = ((tokens, per * DH), F32)
    half_bf16 = ((tokens, per * DH), BF16)
    square = (per, 2, BLOCK, BLOCK)
    mask = ((2, BLOCK, BLOCK), F32)
    scratch_terms = (pltpu.VMEM((heads, DH, DH), F32), pltpu.VMEM((8, DH), F32))

    loc, scans = [], []
    for c in chunks:
        outs = (message, message, states)
        scratch = scratch_terms
        body = functools.partial(k1_body, k, c * heads, CHUNKS)
        if c == 0:
            outs += (((32, tokens), F32), ((tokens, DH), F32)) + (chunk_bf16,) * (2 * CHUNKS)
            scratch += (pltpu.VMEM(log_decay.shape, F32), pltpu.VMEM((1, tokens), jnp.int32), dma((2 * CHUNKS + 2,)))
            outside = (log_decay, run_start.reshape(1, tokens), key_rows, value_rows)
            out = call(body, (), outs, outside=outside, scratch=scratch)
            rows, cols = out[3:5]
            keys, values = out[5::2], out[6::2]
        else:
            out = call(body, (rows, keys[c], values[c]), outs, scratch=scratch)
        loc.append(out[2])
        scans.append(scan_devices(call, lambda own=out[0]: own, out[1], False, k, count))

    forward = []

    def k2(n):
        c = n // PIECES
        outs = (piece_f32, (square, F32), (square, F32), (square, BF16), ((per, 2, DH, BLOCK), BF16))
        outs += (piece_f32, piece_f32)
        inputs = (query_rows, keys[c], values[c], rows, cols)
        if n == 0:
            outs += (mask, mask)
        else:
            inputs += tuple(forward[0][7:])
        forward.append(call(functools.partial(k2_body, n == 0, n * per, c * heads, per), inputs, outs))

    fillers = range(CHUNKS * PIECES)
    rounds = count.bit_length()
    drive(scans, [functools.partial(k2, n) for n in fillers], rounds)
    middle, newest = {}, {}

    def k3(c, other, state):
        mid = forward[c * PIECES : (c + 1) * PIECES]
        inside = (query_rows, out_grad, loc[c], rows, state)
        inside += tuple(f[i] for i in (0, 4, 5) for f in mid)
        renewed = {len(inside) + i: 1 + i for i in range(4)} if c in newest else None
        out = call(
            functools.partial(k3_body, k, c * heads, other),
            inside + tuple(newest.get(c, ())),
            (message, chunk_bf16, ((heads, 2, DH, DH), BF16), states, chunk_bf16),
            renewed=renewed,
        )
        middle[c, other], newest[c] = out[0], out[1:]

    ready = by_halves(scans, k3, K3_TURNS)
    late = {c for c in chunks if (c, 0) not in K3_TURNS}
    scans = [scan_devices(call, lambda c=c: middle[c, 0], middle[c, 1], True, k, count) for c in chunks]

    backward = []

    def k4(n):
        c = n // PIECES
        mixgrad, states_low, _, attended = newest[c]
        f = forward[n]
        backward.append(
            call(
                functools.partial(k4_body, n * per, c * heads, per),
                (query_rows, keys[c], values[c], mixgrad, attended, f[1], f[2], f[3], states_low, f[5])
                + ((backward[-1][2],) if n else ()),
                (piece_f32, piece_f32, ((tokens, per * DH), BF16), flat, flat),
                outside=tuple(backward[-1][3:]) if n else (),
                aliases={0: 3, 1: 4} if n else None,
                scratch=(dma((2,)),),
            )
        )

    drive(scans, [functools.partial(k4, n) for n in fillers], rounds, lambda c: k3(c, 0, ready[c][0]) if c in late else None)
    attended, query_grad = backward[-1][3:]
    final = []

    def k5(c, other, state):
        last = c == CHUNKS - 1 and other == 1
        mid = [forward[n] for n in range(c * PIECES, (c + 1) * PIECES)]
        back = [backward[n] for n in range(c * PIECES, (c + 1) * PIECES)]
        inside = (keys[c], values[c], newest[c][2], rows, state)
        inside += tuple(b[0] for b in back) + tuple(b[1] for b in back) + tuple(f[6] for f in mid)
        kept, query_at, options = (), None, {}
        outs = (half_bf16, half_bf16)
        if not final:
            inside += (backward[-1][2],)
            query_at = CHUNKS * heads - per
            outs += (flat,)
            options = {"outside": (query_grad,), "aliases": {0: 2}, "scratch": (dma((1,)),)}
        elif last:
            kept = tuple(f[1:] for f in final)
            inside += tuple(a for f in final for a in f[0][:2])
            outs = (flat, flat)
            half = pltpu.VMEM((tokens, per * DH), BF16)
            options = {"scratch": (half, half, dma((2 * len(kept) + 2 * per,)))}
        body = functools.partial(k5_body, k, c * heads, other, kept, query_at)
        final.append((call(body, inside, outs, **options), c * heads, other))

    by_halves(scans, k5, K5_TURNS)
    return attended, final[0][0][2], *final[-1][0]


def solution(mesh):
    rows = P(("groups", "seq"), None)
    return jax.shard_map(
        local,
        mesh=mesh,
        in_specs=(rows, rows, rows, P(None, ("groups", "seq")), P(("groups", "seq")), rows),
        out_specs=(rows, rows, rows, rows),
        check_vma=False,
    )
```

```python
import functools

import jax
import jax.numpy as jnp
from jax import lax
from jax.experimental import pallas as pl
from jax.experimental.pallas import tpu as pltpu
from jax.sharding import PartitionSpec as P

BLOCK = 256
HALF = 128
DH = 128
EPS = 1e-05
FAR = -1e30
GROUPS = 4
CHUNKS = 2
K3_TURNS = ((0, 0), (0, 1), (1, 1))
K5_TURNS = ((0, 0), (1, 0), (0, 1), (1, 1))
PIECES = 2
F32 = jnp.float32
BF16 = jnp.bfloat16

NN = (((1,), (0,)), ((), ()))
NT = (((1,), (1,)), ((), ()))
TN = (((0,), (0,)), ((), ()))


def mm(a, b, dims=NN):
    return lax.dot_general(a, b, dims, preferred_element_type=F32)


def cut(j):
    return slice(j * DH, (j + 1) * DH)


def block(b):
    return slice(b * BLOCK, (b + 1) * BLOCK)


def group_of(place):
    return ((place[0] & 1) << 1) | ((place[0] >> 1) & 1)


def position(place, backward):
    return ~place[0] if backward else place[0]


SMEM = pl.BlockSpec(memory_space=pltpu.SMEM)
VMEM = pl.BlockSpec(memory_space=pltpu.VMEM)
ANY = pl.BlockSpec(memory_space=pl.ANY)
HBM = pl.BlockSpec(memory_space=pltpu.HBM)


def run(body, scalar, inside, outs, outside=(), after=(), aliases=None, renewed=None, scratch=(), megabytes=8):
    taken = len(inside) + len(outside)

    def kernel(scalar_ref, *refs):
        body(scalar_ref, *refs[:taken], *refs[taken + len(after) :])

    shapes = [pltpu.HBM(o.shape, o.dtype) if isinstance(o, jax.ShapeDtypeStruct) else pltpu.VMEM(*o) for o in outs]
    return pl.pallas_call(
        kernel,
        in_specs=[SMEM] + [VMEM] * len(inside) + [HBM] * len(outside) + [ANY] * len(after),
        out_specs=[HBM if isinstance(o, jax.ShapeDtypeStruct) else VMEM for o in outs],
        out_shape=shapes,
        input_output_aliases={1 + len(inside) + i: o for i, o in (aliases or {}).items()}
        | {1 + i: o for i, o in (renewed or {}).items()},
        scratch_shapes=list(scratch),
        compiler_params=pltpu.CompilerParams(vmem_limit_bytes=megabytes << 20),
    )(scalar, *[pltpu.with_memory_space_constraint(a, pltpu.VMEM) for a in inside],
      *[pltpu.with_memory_space_constraint(a, pltpu.HBM) for a in outside], *after)


def prepare(decay_ref, start_ref, rows_ref, cols_ref):
    tri = (
        lax.broadcasted_iota(jnp.int32, (BLOCK, BLOCK), 0) <= lax.broadcasted_iota(jnp.int32, (BLOCK, BLOCK), 1)
    ).astype(F32)
    for b in range(decay_ref.shape[1] // BLOCK):
        at = block(b)
        starts = jnp.broadcast_to(start_ref[:, at].astype(F32), (8, BLOCK))
        both = jnp.concatenate([decay_ref[:, at], starts], axis=0)
        sums = lax.dot_general(both, tri, NN, precision=lax.Precision.HIGHEST, preferred_element_type=F32)
        cumul, marks = sums[:8], sums[8:]
        last, last_mark = cumul[:, BLOCK - 1 :], marks[:, BLOCK - 1 :]
        entering = jnp.where(marks == 0.0, jnp.exp(cumul), 0.0)
        leaving = jnp.where(marks == last_mark, jnp.exp(last - cumul), 0.0)
        stack = jnp.concatenate([cumul, entering, leaving, marks], axis=0)
        rows_ref[:, at] = stack
        cols_ref[at, :] = jnp.concatenate([stack, jnp.zeros((96, BLOCK), F32)], axis=0).T


def keeps(rows_ref, head):
    enter = rows_ref[8 + head : 9 + head, :]
    k0 = jnp.broadcast_to(enter[:, BLOCK - 1 : BLOCK], (1, DH))
    k1 = jnp.broadcast_to(enter[:, 2 * BLOCK - 1 : 2 * BLOCK], (1, DH))
    return k0, k1


def send_out(place, k, terms_ref, keep_ref, own_ref, send_ref):
    for out, first in ((own_ref, 0), (send_ref, 2 * k)):
        for r in range(2 * k):
            group, j = (first + r) // k, (first + r) % k
            head = (group ^ group_of(place)) * k + j
            out[cut(r), :] = terms_ref[head]
            out[pl.ds(2 * k * DH + r, 1), :] = keep_ref[pl.ds(head, 1), :]
        rest = 8 - 2 * k
        out[2 * k * DH + 2 * k :, :] = jnp.ones((rest, DH), F32)


def turned_half(place, k, i):
    return ((i // k) ^ ((place[0] >> 1) & 1)) * k + i % k


def at_rows(i):
    return pl.ds(pl.multiple_of(i * DH, DH), DH)


def each_half(place, other, work):
    for p in range(2):
        pl.when(((place[0] & 1) ^ other) == p)(functools.partial(work, p))


def k1_body(k, head0, chunks, place, *refs):
    heads = GROUPS * k
    if head0 == 0:
        decay_hbm, start_hbm, key_hbm, value_hbm, own_ref, send_ref, loc_ref, rows_ref, cols_ref = refs[:9]
        copied = refs[9 : 9 + 2 * chunks]
        terms_ref, keep_ref, decay_ref, start_ref, sems = refs[9 + 2 * chunks :]
        loads = [
            pltpu.make_async_copy(decay_hbm, decay_ref, sems.at[0]),
            pltpu.make_async_copy(start_hbm, start_ref, sems.at[1]),
        ]
        for n, target in enumerate(copied):
            source, first = (key_hbm, value_hbm)[n % 2], n // 2 * heads * DH
            loads.append(pltpu.make_async_copy(source.at[:, first : first + heads * DH], target, sems.at[2 + n]))
        for load in loads:
            load.start()
        loads[0].wait()
        loads[1].wait()
        prepare(decay_ref, start_ref, rows_ref, cols_ref)
        loads[2].wait()
        loads[3].wait()
        key_ref, value_ref = copied[:2]
    else:
        rows_ref, key_ref, value_ref, own_ref, send_ref, loc_ref, terms_ref, keep_ref = refs
        loads = []
    for j in range(heads):
        head = head0 + j
        leave = rows_ref[16 + head : 17 + head, :]
        terms = []
        for b in range(2):
            keys = key_ref[block(b), cut(j)].T.astype(F32)
            scaled = (keys * leave[:, block(b)]).astype(BF16)
            terms.append(mm(scaled, value_ref[block(b), cut(j)]))
        k0, k1 = keeps(rows_ref, head)
        loc_ref[j] = terms[0]
        terms_ref[j] = k1 * terms[0] + terms[1]
        keep_ref[j : j + 1, :] = k0 * k1
    send_out(place, k, terms_ref, keep_ref, own_ref, send_ref)
    for load in loads[4:]:
        load.wait()


def make_bias(rows_ref, cols_ref, bias_ref, turned_ref):
    down = lax.broadcasted_iota(jnp.int32, (BLOCK, BLOCK), 0)
    along = lax.broadcasted_iota(jnp.int32, (BLOCK, BLOCK), 1)
    for b in range(2):
        same = cols_ref[block(b), 24:25] == rows_ref[24:25, block(b)]
        bias_ref[b] = jnp.where((down >= along) & same, 0.0, FAR)
        turned_ref[b] = jnp.where((down <= along) & same, 0.0, FAR)


def k2_body(first, head0, base, count, place, query_ref, key_ref, value_ref, rows_ref, cols_ref, *refs):
    if first:
        (within_ref, grid_ref, turned_ref, weighted_ref, scaled_ref, enter_ref, leave_ref,
         bias_ref, bias_turned_ref) = refs
        make_bias(rows_ref, cols_ref, bias_ref, bias_turned_ref)
    else:
        (bias_ref, bias_turned_ref, within_ref, grid_ref, turned_ref, weighted_ref, scaled_ref, enter_ref,
         leave_ref) = refs
    zeros = jnp.zeros((HALF, HALF), F32)
    for j in range(count):
        head = head0 + j
        inner = head - base
        for b in range(2):
            at = block(b)
            query, key = query_ref[at, cut(head)], key_ref[at, cut(inner)]
            cum_row = rows_ref[head : head + 1, at]
            top, low = slice(0, HALF), slice(HALF, BLOCK)
            cum_top = jnp.broadcast_to(cols_ref[b * BLOCK : b * BLOCK + HALF, head : head + 1], (HALF, HALF))
            cum_low = jnp.broadcast_to(cols_ref[b * BLOCK + HALF : (b + 1) * BLOCK, head : head + 1], (HALF, HALF))
            row_top, row_low = cum_row[:, :HALF], cum_row[:, HALF:]

            def decay(difference, limit):
                return jnp.exp(jnp.minimum(difference, limit))

            grid_ref[j, b, top, top] = decay(cum_top - row_top, bias_ref[b, top, top])
            grid_ref[j, b, low, top] = decay(cum_low - row_top, bias_ref[b, low, top])
            grid_ref[j, b, low, low] = decay(cum_low - row_low, bias_ref[b, low, low])
            grid_ref[j, b, top, low] = zeros
            turned_ref[j, b, top, top] = decay(row_top - cum_top, bias_turned_ref[b, top, top])
            turned_ref[j, b, top, low] = decay(row_low - cum_top, bias_turned_ref[b, top, low])
            turned_ref[j, b, low, low] = decay(row_low - cum_low, bias_turned_ref[b, low, low])
            turned_ref[j, b, low, top] = zeros
            weighted = (mm(query, key, NT) * grid_ref[j, b]).astype(BF16)
            weighted_ref[j, b] = (mm(key, query, NT) * turned_ref[j, b]).astype(BF16)
            within_ref[at, cut(j)] = mm(weighted, value_ref[at, cut(inner)])
            enter = rows_ref[8 + head : 9 + head, at]
            scaled_ref[j, b] = (query.T.astype(F32) * enter).astype(BF16)
            enter_ref[at, cut(j)] = jnp.broadcast_to(cols_ref[at, 8 + head : 9 + head], (BLOCK, DH))
            leave_ref[at, cut(j)] = jnp.broadcast_to(cols_ref[at, 16 + head : 17 + head], (BLOCK, DH))


def k3_body(k, head0, other, place, query_ref, grad_ref, loc_ref, rows_ref, state_ref, *refs):
    per = 2 * k
    withins, scaleds, enters, refs = refs[:2], refs[2:4], refs[4:6], refs[6:]
    message_ref, mixgrad_ref, states_ref, back_ref, attended_ref = refs[-5:]
    message_ref[per * DH :, :] = jnp.ones((8, DH), F32)

    def work(p):
        for i in range(per):
            j = p * per + i
            head = head0 + j
            stand = turned_half(place, k, i)
            k0, k1 = keeps(rows_ref, head)
            incoming = state_ref[at_rows(stand), :]
            states = (incoming, k0 * incoming + loc_ref[j])
            backs = []
            for b in range(2):
                at = block(b)
                low = states[b].astype(BF16)
                states_ref[j, b] = low
                mixture = withins[p][at, cut(i)] + mm(query_ref[at, cut(head)], low) * enters[p][at, cut(i)]
                wide = grad_ref[at, cut(head)].astype(F32)
                inverse = lax.rsqrt(jnp.mean(mixture * mixture, axis=1, keepdims=True) + EPS)
                along = jnp.mean(wide * mixture, axis=1, keepdims=True) * inverse
                normed = mixture * inverse
                attended_ref[at, cut(j)] = normed.astype(BF16)
                mixgrad = (inverse * (wide - normed * along)).astype(BF16)
                mixgrad_ref[at, cut(j)] = mixgrad
                backs.append(mm(scaleds[p][i, b], mixgrad))
            back_ref[j] = backs[1]
            message_ref[at_rows(stand), :] = k0 * backs[1] + backs[0]
            message_ref[pl.ds(per * DH + stand, 1), :] = k0 * k1

    each_half(place, other, work)


def columns(ref, first, count):
    return ref.at[:, first * DH : (first + count) * DH]


def k4_body(head0, base, count, place, query_ref, key_ref, value_ref, mixgrad_ref, attended_ref, grid_ref,
            turned_ref, weighted_ref, states_ref, enter_ref, *refs):
    later = head0 > 0
    key_part_ref, value_part_ref, query_grad_ref, attended_hbm, query_grad_hbm, sems = refs[3 * later :]
    inner0 = head0 - base
    copies = [
        pltpu.make_async_copy(
            columns(attended_ref, inner0, count), columns(attended_hbm, head0, count), sems.at[0]
        )
    ]
    if later:
        copies.append(
            pltpu.make_async_copy(refs[0], columns(query_grad_hbm, head0 - count, count), sems.at[1])
        )
    for copy in copies:
        copy.start()
    for j in range(count):
        head = head0 + j
        inner = head - base
        for b in range(2):
            at = block(b)
            mixgrad = mixgrad_ref[at, cut(inner)]
            value = value_ref[at, cut(inner)]
            masked = (mm(mixgrad, value, NT) * grid_ref[j, b]).astype(BF16)
            query_grad_ref[at, cut(j)] = (
                mm(masked, key_ref[at, cut(inner)]) + mm(mixgrad, states_ref[inner, b], NT) * enter_ref[at, cut(j)]
            ).astype(BF16)
            turned = (mm(value, mixgrad, NT) * turned_ref[j, b]).astype(BF16)
            key_part_ref[at, cut(j)] = mm(turned, query_ref[at, cut(head)])
            value_part_ref[at, cut(j)] = mm(weighted_ref[j, b], mixgrad)
    for copy in copies:
        copy.wait()


def k5_body(k, head0, other, kept, query_at, place, key_ref, value_ref, back_ref, rows_ref, state_ref, *refs):
    per = 2 * k
    key_parts, value_parts, leaves, refs = refs[:2], refs[2:4], refs[4:6], refs[6:]
    left, refs = refs[: 2 * len(kept)], refs[2 * len(kept) :]
    if query_at is not None:
        query_ref, _, key_grad_ref, value_grad_ref, query_hbm, sems = refs
    elif kept:
        key_hbm, value_hbm, key_grad_ref, value_grad_ref, sems = refs
    else:
        key_grad_ref, value_grad_ref = refs

    def ship(source, target, sem):
        copy = pltpu.make_async_copy(source, target, sems.at[sem])
        copy.start()
        return copy

    copies = []
    if query_at is not None:
        copies.append(ship(query_ref, columns(query_hbm, query_at, per), 0))
    for n, (base, half) in enumerate(kept):
        start = pl.multiple_of((base + ((place[0] & 1) ^ half) * per) * DH, DH)
        copies.append(ship(left[2 * n], key_hbm.at[:, pl.ds(start, per * DH)], 2 * n))
        copies.append(ship(left[2 * n + 1], value_hbm.at[:, pl.ds(start, per * DH)], 2 * n + 1))

    def work(p):
        ours = []
        for i in range(per):
            j = p * per + i
            k0, k1 = keeps(rows_ref, head0 + j)
            outgoing = state_ref[at_rows(turned_half(place, k, i)), :]
            afters = (k1 * outgoing + back_ref[j], outgoing)
            for b in range(2):
                at = block(b)
                low = afters[b].astype(BF16)
                leave = leaves[p][at, cut(i)]
                key_grad_ref[at, cut(i)] = (
                    key_parts[p][at, cut(i)] + mm(value_ref[at, cut(j)], low, NT) * leave
                ).astype(BF16)
                value_grad_ref[at, cut(i)] = (
                    value_parts[p][at, cut(i)] + mm(key_ref[at, cut(j)], low) * leave
                ).astype(BF16)
            if kept:
                sem = 2 * len(kept) + 2 * i
                ours.append(ship(columns(key_grad_ref, i, 1), columns(key_hbm, head0 + j, 1), sem))
                ours.append(ship(columns(value_grad_ref, i, 1), columns(value_hbm, head0 + j, 1), sem + 1))
        for copy in ours:
            copy.wait()

    each_half(place, other, work)
    for copy in copies:
        copy.wait()


def joined(later, got_ref, held_ref, heads, j):
    one = slice(heads * DH + j, heads * DH + j + 1)
    a_got, a_held = got_ref[one, :], held_ref[one, :]
    state = jnp.where(later, a_held, 1.0) * got_ref[cut(j), :] + jnp.where(later, 1.0, a_got) * held_ref[cut(j), :]
    return state, a_got * a_held


def before(later, got_ref, prefix_ref, k, j):
    one = slice(k * DH + j, k * DH + j + 1)
    a_got = got_ref[one, :]
    if prefix_ref is None:
        return jnp.where(later, 1.0, 0.0) * got_ref[cut(j), :], jnp.where(later, a_got, 1.0)
    a = prefix_ref[one, :]
    state = jnp.where(later, a, 0.0) * got_ref[cut(j), :] + prefix_ref[cut(j), :]
    return state, jnp.where(later, a * a_got, a)


def put(out, heads, j, value):
    out[cut(j), :], out[heads * DH + j : heads * DH + j + 1, :] = value


def c1_body(turn, k, place, own_ref, got_ref, keep_ref, send_ref):
    later = (position(place, turn) & 1) == 1
    for out in (keep_ref, send_ref):
        out[k * DH :, :] = jnp.ones((8, DH), F32)
    for j in range(2 * k):
        put(keep_ref if j < k else send_ref, k, j % k, joined(later, got_ref, own_ref, 2 * k, j))


def c2_body(turn, k, place, own_ref, got_ref, total_ref):
    later = (position(place, turn) & 2) == 2
    total_ref[k * DH :, :] = jnp.ones((8, DH), F32)
    for j in range(k):
        put(total_ref, k, j, joined(later, got_ref, own_ref, k, j))


def cz_body(turn, k, bit, first, place, *refs):
    total_ref, got_ref = refs[:2]
    prefix_ref = None if first else refs[2]
    new_total_ref, new_prefix_ref = refs[-2:]
    later = (position(place, turn) & bit) == bit
    for out in (new_total_ref, new_prefix_ref):
        out[k * DH :, :] = jnp.ones((8, DH), F32)
    for j in range(k):
        put(new_total_ref, k, j, joined(later, got_ref, total_ref, k, j))
        put(new_prefix_ref, k, j, before(later, got_ref, prefix_ref, k, j))


def c3_body(turn, k, bit, first, place, *refs):
    got_ref = refs[0]
    prefix_ref = None if first else refs[1]
    own_ref, chip_ref, mine_ref, send_ref = refs[-4:]
    later = (position(place, turn) & bit) == bit
    upper = (position(place, turn) & 2) == 2
    for j in range(k):
        at, one = cut(j), slice(k * DH + j, k * DH + j + 1)
        prefix, _ = before(later, got_ref, prefix_ref, k, j)
        mine_ref[at, :] = jnp.where(upper, chip_ref[one, :], 1.0) * prefix + jnp.where(upper, 1.0, 0.0) * chip_ref[at, :]
        send_ref[at, :] = jnp.where(upper, 1.0, own_ref[one, :]) * prefix + jnp.where(upper, 0.0, 1.0) * own_ref[at, :]


def c4_body(turn, k, place, half_ref, got_half_ref, own_ref, got_ref, mine_ref, send_ref):
    later = (position(place, turn) & 1) == 1
    for j in range(2 * k):
        at, one = cut(j), slice(2 * k * DH + j, 2 * k * DH + j + 1)
        chip = half_ref[cut(j), :] if j < k else got_half_ref[cut(j - k), :]
        mine_ref[at, :] = jnp.where(later, got_ref[one, :], 1.0) * chip + jnp.where(later, 1.0, 0.0) * got_ref[at, :]
        send_ref[at, :] = jnp.where(later, 1.0, own_ref[one, :]) * chip + jnp.where(later, 0.0, 1.0) * own_ref[at, :]


def exchange(x, bit, count):
    return lax.ppermute(x, "seq", [(i, i ^ bit) for i in range(count)])


class Order:
    def __init__(self, place):
        self.place, self.last = place, ()

    def __call__(self, body, inside, outs, **options):
        taken = [id(a) for a in (*options.get("outside", ()), *inside)]
        after = tuple(a for a in self.last if id(a) not in taken)
        out = run(body, self.place, inside, outs, after=after, **options)
        self.last = (out[0],)
        return out


def scan_devices(call, own, send, turn, k, count):
    half = ((k * DH + 8, DH), F32)
    got = exchange(send, 1, count)
    yield
    own = own()
    chip, chip_send = call(functools.partial(c1_body, turn, k), (own, got), (half, half))
    chip_got = exchange(chip_send, 2, count)
    yield
    (total,) = call(functools.partial(c2_body, turn, k), (chip, chip_got), (half,))
    prefix = ()
    bit = 4
    while bit < count:
        got_total = exchange(total, bit, count)
        yield
        if bit * 2 < count:
            body = functools.partial(cz_body, turn, k, bit, not prefix)
            total, *prefix = call(body, (total, got_total, *prefix), (half, half))
        else:
            body = functools.partial(c3_body, turn, k, bit, not prefix)
            mine, mine_send = call(body, (got_total, *prefix, chip, chip_got), (((k * DH, DH), F32),) * 2)
        bit *= 2
    mine_got = exchange(mine_send, 2, count)
    yield
    body = functools.partial(c4_body, turn, k)
    state, state_send = call(body, (mine, mine_got, own, got), (((2 * k * DH, DH), F32),) * 2)
    yield state, exchange(state_send, 1, count)


def drive(scans, fillers, rounds, late=None):
    fillers = list(fillers)
    for step in range(rounds):
        for c, scan in enumerate(scans):
            if step == 1 and late:
                late(c)
            next(scan)
        pieces = int(step > 0) if late else (step > 1) + (step == rounds - 2)
        for _ in range(min(pieces, len(fillers))):
            fillers.pop(0)()
    for filler in fillers:
        filler()


def by_halves(scans, half, turns):
    ready = {}
    for c, other in turns:
        for n in range(c + 1 + (len(ready) > 0 and c + 1 < len(scans))):
            if n not in ready:
                ready[n] = next(scans[n])
        half(c, other, ready[c][other])
    return ready


def local(query_rows, key_rows, value_rows, log_decay, run_start, out_grad):
    all_heads = log_decay.shape[0]
    tokens, width = query_rows.shape
    count = lax.axis_size("seq")
    seat = lax.axis_index("seq")
    call = Order(seat.reshape(1))
    heads = all_heads // CHUNKS
    k = heads // GROUPS
    per = heads // PIECES
    chunks = range(CHUNKS)
    dma = pltpu.SemaphoreType.DMA
    message = ((2 * k * DH + 8, DH), F32)
    states = ((heads, DH, DH), F32)
    flat = jax.ShapeDtypeStruct((tokens, width), BF16)
    chunk_bf16 = ((tokens, heads * DH), BF16)
    piece_f32 = ((tokens, per * DH), F32)
    half_bf16 = ((tokens, per * DH), BF16)
    square = (per, 2, BLOCK, BLOCK)
    mask = ((2, BLOCK, BLOCK), F32)
    scratch_terms = (pltpu.VMEM((heads, DH, DH), F32), pltpu.VMEM((8, DH), F32))

    loc, scans = [], []
    for c in chunks:
        outs = (message, message, states)
        scratch = scratch_terms
        body = functools.partial(k1_body, k, c * heads, CHUNKS)
        if c == 0:
            outs += (((32, tokens), F32), ((tokens, DH), F32)) + (chunk_bf16,) * (2 * CHUNKS)
            scratch += (pltpu.VMEM(log_decay.shape, F32), pltpu.VMEM((1, tokens), jnp.int32), dma((2 * CHUNKS + 2,)))
            outside = (log_decay, run_start.reshape(1, tokens), key_rows, value_rows)
            out = call(body, (), outs, outside=outside, scratch=scratch)
            rows, cols = out[3:5]
            keys, values = out[5::2], out[6::2]
        else:
            out = call(body, (rows, keys[c], values[c]), outs, scratch=scratch)
        loc.append(out[2])
        scans.append(scan_devices(call, lambda own=out[0]: own, out[1], False, k, count))

    forward = []

    def k2(n):
        c = n // PIECES
        outs = (piece_f32, (square, F32), (square, F32), (square, BF16), ((per, 2, DH, BLOCK), BF16))
        outs += (piece_f32, piece_f32)
        inputs = (query_rows, keys[c], values[c], rows, cols)
        if n == 0:
            outs += (mask, mask)
        else:
            inputs += tuple(forward[0][7:])
        forward.append(call(functools.partial(k2_body, n == 0, n * per, c * heads, per), inputs, outs))

    fillers = range(CHUNKS * PIECES)
    rounds = count.bit_length()
    drive(scans, [functools.partial(k2, n) for n in fillers], rounds)
    middle, newest = {}, {}

    def k3(c, other, state):
        mid = forward[c * PIECES : (c + 1) * PIECES]
        inside = (query_rows, out_grad, loc[c], rows, state)
        inside += tuple(f[i] for i in (0, 4, 5) for f in mid)
        renewed = {len(inside) + i: 1 + i for i in range(4)} if c in newest else None
        out = call(
            functools.partial(k3_body, k, c * heads, other),
            inside + tuple(newest.get(c, ())),
            (message, chunk_bf16, ((heads, 2, DH, DH), BF16), states, chunk_bf16),
            renewed=renewed,
        )
        middle[c, other], newest[c] = out[0], out[1:]

    ready = by_halves(scans, k3, K3_TURNS)
    late = {c for c in chunks if (c, 0) not in K3_TURNS}
    scans = [scan_devices(call, lambda c=c: middle[c, 0], middle[c, 1], True, k, count) for c in chunks]

    backward = []

    def k4(n):
        c = n // PIECES
        mixgrad, states_low, _, attended = newest[c]
        f = forward[n]
        backward.append(
            call(
                functools.partial(k4_body, n * per, c * heads, per),
                (query_rows, keys[c], values[c], mixgrad, attended, f[1], f[2], f[3], states_low, f[5])
                + ((backward[-1][2],) if n else ()),
                (piece_f32, piece_f32, ((tokens, per * DH), BF16), flat, flat),
                outside=tuple(backward[-1][3:]) if n else (),
                aliases={0: 3, 1: 4} if n else None,
                scratch=(dma((2,)),),
            )
        )

    drive(scans, [functools.partial(k4, n) for n in fillers], rounds, lambda c: k3(c, 0, ready[c][0]) if c in late else None)
    attended, query_grad = backward[-1][3:]
    final = []

    def k5(c, other, state):
        last = c == CHUNKS - 1 and other == 1
        mid = [forward[n] for n in range(c * PIECES, (c + 1) * PIECES)]
        back = [backward[n] for n in range(c * PIECES, (c + 1) * PIECES)]
        inside = (keys[c], values[c], newest[c][2], rows, state)
        inside += tuple(b[0] for b in back) + tuple(b[1] for b in back) + tuple(f[6] for f in mid)
        kept, query_at, options = (), None, {}
        outs = (half_bf16, half_bf16)
        if not final:
            inside += (backward[-1][2],)
            query_at = CHUNKS * heads - per
            outs += (flat,)
            options = {"outside": (query_grad,), "aliases": {0: 2}, "scratch": (dma((1,)),)}
        elif last:
            kept = tuple(f[1:] for f in final)
            inside += tuple(a for f in final for a in f[0][:2])
            outs = (flat, flat)
            half = pltpu.VMEM((tokens, per * DH), BF16)
            options = {"scratch": (half, half, dma((2 * len(kept) + 2 * per,)))}
        body = functools.partial(k5_body, k, c * heads, other, kept, query_at)
        final.append((call(body, inside, outs, **options), c * heads, other))

    by_halves(scans, k5, K5_TURNS)
    return attended, final[0][0][2], *final[-1][0]


def solution(mesh):
    rows = P(("groups", "seq"), None)
    return jax.shard_map(
        local,
        mesh=mesh,
        in_specs=(rows, rows, rows, P(None, ("groups", "seq")), P(("groups", "seq")), rows),
        out_specs=(rows, rows, rows, rows),
        check_vma=False,
    )
```
